32 devices in a mesh: groups: 2 (over x), ctx: 16 (over z, y, core).
Axes of the slice: x: 2, y: 2, z: 4, core: 2. Of those that a mesh axis runs over, the one named last changes fastest.
Arguments:
- queries: bfloat16 [8192, 3072], P(('groups', 'ctx')), parts along dimension 0, may hold values from -60 to 60
- key_states: bfloat16 [8192, 3072], P(('groups', 'ctx')), parts along dimension 0, may hold values from -6 to 6
- value_states: bfloat16 [8192, 3072], P(('groups', 'ctx')), parts along dimension 0, may hold values from -6 to 6
- stretch_lengths: int32 [32], P('groups'), parts along dimension 0, may hold values from 1 to 512, 4096 in all
- stretch_mask: int32 [32, 16], P('groups'), parts along dimension 0, may hold values from 0 to 1, as said below
Outputs:
- attended: bfloat16 [8192, 3072], P(('groups', 'ctx')), parts along dimension 0
The draws below stay inside these ranges and needn't reach their ends.
There are 2 independent parts, one for each index of `groups`. The reference program is written for one: setup_inputs(seed, part) draws one part's arguments, and reference() takes and returns one part's arrays. A program takes and returns all parts, laid end to end along the dimension named above; each array names one. Nothing has to cross between parts.
Inputs may be any that keep to these rules, and one draw needn't show every extreme that they name: `stretch_lengths`: every stretch holds 1 to 512 tokens, at least one exactly 512; together 4096. stretch_mask[a, b] is 1 where b = a and 0 where b > a or b < a - 1.
All inputs are finite; a program needn't handle non-finite values.
Results may differ from the reference program's by a relative error of at most 0.0035.
Values may be sent and summed in bfloat16 or wider, within the bound.
No kernel may reach another device: no remote copies, remote signals or barrier semaphores. Data moves between devices by JAX's collectives and lax.ppermute only.
A program may use at most 192 MiB of HBM per device.

```python
import math
import jax
import jax.numpy as jnp
import numpy as np
from jax import lax

HEADS = 24
HEAD = 128
TOK_DEV = 256
MAXLEN = 512
WIN = 1
TOKENS = 4096
NCH = 16
REACH_BACK = 4
REACH_FWD = 2


def drawn_fields(key):
    shape = (TOKENS, HEADS * HEAD)
    key_part = jnp.clip(jax.random.normal(jax.random.fold_in(key, 111), shape, jnp.float32), -6.0, 6.0)
    query_part = jnp.clip(2.0 * jax.random.normal(jax.random.fold_in(key, 112), shape, jnp.float32), -12.0, 12.0)
    return (query_part, key_part)


def draw_queries(key, part):
    return drawn_fields(key)[0].astype(jnp.bfloat16)


def draw_key_states(key, part):
    return drawn_fields(key)[1].astype(jnp.bfloat16)


def draw_stretch_mask(key, part):
    row_ids = jnp.arange(NCH, dtype=jnp.int32)[:, None]
    col_ids = jnp.arange(NCH, dtype=jnp.int32)[None, :]
    coin = jax.random.randint(jax.random.fold_in(key, 121), (NCH, NCH), 0, 4)
    earlier = (col_ids < row_ids) & (col_ids >= row_ids - WIN) & (coin > 0)
    return jnp.where(row_ids == col_ids, 1, jnp.where(earlier, 1, 0)).astype(jnp.int32)


def block_levels(rng, dims, split, smallest, high):
    gain, own = 1.0, jax.random.fold_in(rng, 6)
    for axis_at, parts in split:
        heights = jnp.exp(jax.random.uniform(jax.random.fold_in(own, axis_at), (parts,), jnp.float32, smallest / len(split), high / len(split)))
        gain = gain * jnp.repeat(heights, dims[axis_at] // parts).reshape([-1 if axis == axis_at else 1 for axis in range(len(dims))])
    return gain


def split_up(count, total, reach, slope):
    portions = [(1 << 20) // math.isqrt(rank ** slope) + 1 for rank in range(2, count + 1)]
    surplus, counts = total - reach - (count - 1), [1] * (count - 1)
    while surplus > 0:
        candidates = [i for i in range(count - 1) if counts[i] < reach]
        whole, left = sum([portions[i] for i in candidates]), surplus
        for i in candidates:
            more = min(reach - counts[i], max(1, left * portions[i] // whole), surplus)
            counts[i] = counts[i] + more
            surplus = surplus - more
    return np.array([reach] + counts)


def uneven_parts(rng, amount, total, most, skew):
    if amount == 2:
        one = jax.random.randint(rng, (), max(1, total - most), min(most, total - 1) + 1)
        return jnp.stack([one, total - one])
    sizes = jnp.asarray(split_up(amount, total, most, skew), jnp.int32)
    twos = (amount - 1) // 2
    giver, receiver = sizes[1:1 + 2 * twos:2], sizes[2:2 + 2 * twos:2]
    room = jnp.minimum(giver - 1, most - receiver)
    passed = jax.random.randint(jax.random.fold_in(rng, 1), (twos,), 0, 1 << 20) % (room + 1)
    sizes = sizes.at[1:1 + 2 * twos:2].set(giver - passed).at[2:2 + 2 * twos:2].set(receiver + passed)
    return sizes[jax.random.permutation(jax.random.fold_in(rng, 2), amount)]


def centred(rng, extent, width, bound, cuts=(), kind=jnp.bfloat16):
    entries = jax.random.normal(rng, extent, jnp.float32) * width
    if len(cuts) > 0:
        entries = block_levels(rng, extent, cuts, -0.22, 0.18) * entries
    return jnp.clip(entries, min=-bound, max=bound).astype(kind)


def setup_inputs(seed: int = 0, part: int = 0) -> dict:
    splits = jax.random.split(jax.random.key(seed), 6)
    own_keys = jax.random.split(jax.random.fold_in(splits[5], part), 6)
    queries = draw_queries(jax.random.fold_in(jax.random.fold_in(splits[5], part), 71), part)
    key_states = draw_key_states(jax.random.fold_in(jax.random.fold_in(splits[5], part), 71), part)
    value_states = centred(own_keys[2], (TOKENS, HEADS * HEAD), 1.0, 6.0, ((0, 16),))
    stretch_lengths = uneven_parts(own_keys[3], NCH, TOKENS, MAXLEN, 2).astype(jnp.int32)
    stretch_mask = draw_stretch_mask(jax.random.fold_in(jax.random.fold_in(splits[5], part), 71), part)
    return dict(queries=queries, key_states=key_states, value_states=value_states, stretch_lengths=stretch_lengths, stretch_mask=stretch_mask)


def stretch_ids(positions, stretch_lengths):
    stretch_ends = jnp.cumsum(stretch_lengths).astype(jnp.int32)
    counted = lax.optimization_barrier(jnp.sum((positions[:, None] >= stretch_ends[None, :]).astype(jnp.int32), axis=1))
    return jnp.minimum(counted, stretch_lengths.shape[0] - 1).astype(jnp.int32)

def reference(queries, key_states, value_states, stretch_lengths, stretch_mask):
    feature_width = queries.shape[1]
    head_count = feature_width // HEAD
    lead_rows = REACH_BACK * TOK_DEV
    span_rows = (REACH_BACK + 1 + REACH_FWD) * TOK_DEV
    key_padded = jnp.pad(key_states, ((lead_rows, REACH_FWD * TOK_DEV), (0, 0)))
    value_padded = jnp.pad(value_states, ((lead_rows, REACH_FWD * TOK_DEV), (0, 0)))
    scale = 1.0 / math.sqrt(HEAD)

    def one_block(block):
        first = (block * TOK_DEV).astype(jnp.int32)
        query_block = lax.dynamic_slice_in_dim(queries, first, TOK_DEV, 0)
        key_block = lax.dynamic_slice_in_dim(key_padded, first, span_rows, 0)
        value_block = lax.dynamic_slice_in_dim(value_padded, first, span_rows, 0)
        query_pos = first + jnp.arange(TOK_DEV, dtype=jnp.int32)
        key_pos = first - lead_rows + jnp.arange(span_rows, dtype=jnp.int32)
        query_stretch = stretch_ids(query_pos, stretch_lengths)
        key_stretch = stretch_ids(jnp.maximum(key_pos, 0), stretch_lengths)
        allowed = stretch_mask[query_stretch][:, key_stretch] > 0
        inside = (key_pos >= 0) & (key_pos < TOKENS)
        allowed = allowed & inside[None, :]
        query_heads = query_block.reshape(TOK_DEV, head_count, HEAD).astype(jnp.float32)
        key_heads = key_block.reshape(span_rows, head_count, HEAD).astype(jnp.float32)
        value_heads = value_block.reshape(span_rows, head_count, HEAD).astype(jnp.float32)
        scores = jnp.einsum('qhd,khd->hqk', query_heads, key_heads) * scale
        scores = jnp.where(allowed[None], scores, -jnp.inf)
        top_score = lax.optimization_barrier(jnp.max(scores, axis=2, keepdims=True))
        weights = jnp.exp(scores - top_score)
        totals = lax.optimization_barrier(jnp.sum(weights, axis=2))
        rounded = lax.optimization_barrier(weights.astype(jnp.bfloat16)).astype(jnp.float32)
        summed = jnp.einsum('hqk,khd->qhd', rounded, value_heads)
        normed = summed / totals.T[:, :, None]
        return normed.reshape(TOK_DEV, feature_width).astype(jnp.bfloat16)
    blocks = lax.map(one_block, jnp.arange(TOKENS // TOK_DEV, dtype=jnp.int32))
    return blocks.reshape(TOKENS, feature_width)
```

```python
import functools
import math

import jax
import jax.numpy as jnp
from jax import lax
from jax.experimental import pallas as pl
from jax.experimental.pallas import tpu as pltpu
from jax.sharding import PartitionSpec as P

HEAD = 128
MAXLEN = 512
WIN = 1
LEVEL = 4
GROUPS = 3
NEG = -1e30
ANY = pl.BlockSpec(memory_space=pl.ANY)
VMEM = pl.BlockSpec(memory_space=pltpu.VMEM)
SMEM = pl.BlockSpec(memory_space=pltpu.SMEM)


def swap(value, bits):
    return lax.ppermute(value, "ctx", [(i, i ^ bits) for i in range(lax.axis_size("ctx"))])


def shift(value, steps):
    count = lax.axis_size("ctx")
    return lax.ppermute(
        value, "ctx", [(i, i + steps) for i in range(count) if 0 <= i + steps < count]
    )


def run_copies(pairs, sems):
    copies = [pltpu.make_async_copy(a, b, sems.at[n]) for n, (a, b) in enumerate(pairs)]
    for c in copies:
        c.start()
    for c in copies:
        c.wait()


def cost(nbytes, flops=0):
    return pl.CostEstimate(flops=flops, bytes_accessed=nbytes, transcendentals=0)


def col(index, unit):
    return pl.multiple_of(index * unit, unit)


def pack_kv(keys, values, group, width, slab, labels, name):
    rows = keys.shape[0]

    def kernel(k, v, *rest):
        outs, sems = rest[:-1], rest[-1]
        j = lax.rem(lax.axis_index("ctx"), LEVEL)
        pairs = []
        for out, d in zip(outs, labels):
            c = pl.multiple_of((j ^ d) * slab + group * width, 128)
            pairs.append((k.at[:, pl.ds(c, width)], out.at[:, pl.ds(0, width)]))
            pairs.append((v.at[:, pl.ds(c, width)], out.at[:, pl.ds(width, width)]))
        run_copies(pairs, sems)

    return pl.pallas_call(
        kernel,
        out_shape=[jax.ShapeDtypeStruct((rows, 2 * width), keys.dtype)] * len(labels),
        in_specs=[ANY, ANY],
        out_specs=[VMEM] * len(labels),
        scratch_shapes=[pltpu.SemaphoreType.DMA((2 * len(labels),))],
        cost_estimate=cost(8 * rows * width * len(labels)),
        name=name,
    )(keys, values)


def pack_q(queries, slab):
    rows = queries.shape[0]
    labels = range(1, LEVEL)

    def kernel(q, *rest):
        outs, sems = rest[:-1], rest[-1]
        j = lax.rem(lax.axis_index("ctx"), LEVEL)
        run_copies(
            [(q.at[:, pl.ds(col(j ^ d, slab), slab)], out) for out, d in zip(outs, labels)], sems
        )

    return pl.pallas_call(
        kernel,
        out_shape=[jax.ShapeDtypeStruct((rows, slab), queries.dtype)] * len(labels),
        in_specs=[ANY],
        out_specs=[VMEM] * len(labels),
        scratch_shapes=[pltpu.SemaphoreType.DMA((len(labels),))],
        cost_estimate=cost(4 * rows * slab * len(labels)),
        name="pack_q",
    )(queries)


def pack_z(own, swapped, ahead):
    rows, width = own.shape

    def kernel(o, *rest):
        pieces, fwd, back, sems = [o, *rest[: LEVEL - 1]], *rest[LEVEL - 1 :]
        j = lax.rem(lax.axis_index("ctx"), LEVEL)
        copies = [
            pltpu.make_async_copy(pieces[d], fwd.at[d - 1], sems.at[d - 1])
            for d in range(1, LEVEL)
        ]
        for c in copies:
            c.start()
        for b in range(ahead):
            for d in range(LEVEL):
                @pl.when((j ^ b) == d)
                def _():
                    pltpu.make_async_copy(pieces[d], back.at[b], sems.at[LEVEL - 1 + b]).start()
        for c in copies:
            c.wait()
        for b in range(ahead):
            pltpu.make_async_copy(o, back.at[b], sems.at[LEVEL - 1 + b]).wait()

    return pl.pallas_call(
        kernel,
        out_shape=[
            jax.ShapeDtypeStruct((LEVEL - 1, rows, width), own.dtype),
            jax.ShapeDtypeStruct((ahead, rows, width), own.dtype),
        ],
        in_specs=[ANY] * LEVEL,
        out_specs=[VMEM, VMEM],
        scratch_shapes=[pltpu.SemaphoreType.DMA((LEVEL - 1 + ahead,))],
        cost_estimate=cost(4 * rows * width * (LEVEL - 1 + ahead)),
        name="pack_z",
    )(own, *swapped)


def attention(lengths, mask, queries, q_swapped, own, swapped, prev_own, prev_rest, ahead, group, width, slab):
    rows = queries.shape[0]
    heads = width // HEAD
    stretches = lengths.shape[0]
    next_blocks = ahead.shape[0]
    key_blocks = 2 * LEVEL + next_blocks
    key_rows = key_blocks * rows
    tile = 256
    factor = math.log2(math.e) / math.sqrt(HEAD)

    def kernel(len_ref, mask_ref, q, *rest):
        qx, rest = rest[: LEVEL - 1], rest[LEVEL - 1 :]
        level, rest = rest[:LEVEL], rest[LEVEL:]
        p_own, p_rest, nxt, rest = rest[0], rest[1], rest[2], rest[3:]
        outs, (ks, vs, vt, qs, os, acc, sems, out_sems) = rest[:LEVEL], rest[LEVEL:]
        me = lax.axis_index("ctx")
        j = lax.rem(me, LEVEL)
        z = me // LEVEL
        pairs = []

        def kv(src, block):
            at = pl.ds(pl.multiple_of(block * rows, rows), rows)
            pairs.append((src.at[:, pl.ds(0, width)], ks.at[at, :]))
            pairs.append((src.at[:, pl.ds(width, width)], vs.at[at, :]))

        for d in range(LEVEL):
            kv(level[d], LEVEL + (j ^ d))
            kv(p_own if d == 0 else p_rest.at[d - 1], j ^ d)
            at = pl.ds(pl.multiple_of((j ^ d) * rows, rows), rows)
            if d == 0:
                c = pl.multiple_of(j * slab + group * width, 128)
                pairs.append((q.at[:, pl.ds(c, width)], qs.at[at, :]))
            else:
                pairs.append((qx[d - 1].at[:, pl.ds(group * width, width)], qs.at[at, :]))
        for b in range(next_blocks):
            kv(nxt.at[b], 2 * LEVEL + b)
        run_copies(pairs, sems)

        @pl.loop(0, key_rows // tile)
        def _(i):
            at = pl.ds(pl.multiple_of(i * tile, tile), tile)
            for h in range(heads):
                vt[h, :, at] = vs[at, h * HEAD : (h + 1) * HEAD].T

        base = (z - 1) * LEVEL * rows
        lane = lax.broadcasted_iota(jnp.int32, (1, rows), 1)
        sub = lax.broadcasted_iota(jnp.int32, (1, 8, rows), 1)

        @pl.loop(0, LEVEL)
        def _(b):
            first = (LEVEL + b) * rows
            at = pl.ds(pl.multiple_of(b * rows, rows), rows)
            pos = lane + first

            def scan(a, carry):
                start, before, lo, hi, lo_min, hi_max = carry
                length = len_ref[a]
                back = jnp.where(mask_ref[a, jnp.maximum(a - 1, 0)] > 0, before, 0)
                end = start + length
                here = pos >= start
                lo = jnp.where(here, start - back, lo)
                hi = jnp.where(here, end, hi)
                lo_min = jnp.where(start <= first, start - back, lo_min)
                hi_max = jnp.where(start < first + rows, end, hi_max)
                return end, length, lo, hi, lo_min, hi_max

            zero = jnp.zeros_like(pos)
            none = jnp.int32(0)
            _, _, lo, hi, lo_min, hi_max = lax.fori_loop(
                0, stretches, scan, (-base, none, zero, zero, none, none)
            )
            start = jnp.maximum(lo_min, 0) // HEAD * HEAD
            tiles = (hi_max - start + tile - 1) // tile
            start = jnp.minimum(start, key_rows - tiles * tile)
            lo8 = lo[None] - sub
            hi8 = hi[None] - sub
            for h in range(heads):
                acc[h] = jnp.zeros_like(acc[h])

            def step(t, carry):
                k0 = pl.multiple_of(start + t * tile, HEAD)
                offs = lax.broadcasted_iota(jnp.int32, (tile // 8, 1, 1), 0) * 8 + k0
                valid = (lo8 <= offs) & (hi8 > offs)
                new = []
                for h in range(heads):
                    top, total = carry[h]
                    hc = slice(h * HEAD, (h + 1) * HEAD)
                    s = lax.dot_general(
                        ks[pl.ds(k0, tile), hc],
                        qs[at, hc],
                        (((1,), (1,)), ((), ())),
                        preferred_element_type=jnp.float32,
                    )
                    s = jnp.where(valid, s.reshape(tile // 8, 8, rows), NEG).reshape(tile, rows)
                    top_new = jnp.maximum(top, jnp.max(s, axis=0, keepdims=True))
                    p = jnp.exp2((s - top_new) * factor)
                    alpha = jnp.exp2((top - top_new) * factor)
                    total = total * alpha + jnp.sum(p, axis=0, keepdims=True)
                    acc[h] = acc[h] * alpha + jnp.dot(
                        vt[h, :, pl.ds(k0, tile)],
                        p.astype(jnp.bfloat16),
                        preferred_element_type=jnp.float32,
                    )
                    new.append((top_new, total))
                return tuple(new)

            init = (jnp.full((1, rows), NEG, jnp.float32), jnp.zeros((1, rows), jnp.float32))
            ends = lax.fori_loop(0, tiles, step, (init,) * heads)
            for h in range(heads):
                normed = acc[h] / ends[h][1]
                os[at, h * HEAD : (h + 1) * HEAD] = normed.T.astype(jnp.bfloat16)

        run_copies(
            [
                (os.at[pl.ds(pl.multiple_of((j ^ d) * rows, rows), rows), :], outs[d])
                for d in range(LEVEL)
            ],
            out_sems,
        )

    bf = jnp.bfloat16
    n_copies = 2 * (2 * LEVEL + next_blocks) + LEVEL
    return pl.pallas_call(
        kernel,
        out_shape=[jax.ShapeDtypeStruct((rows, width), bf)] * LEVEL,
        in_specs=[SMEM, SMEM] + [ANY] * (2 * LEVEL + 3),
        out_specs=[ANY] * LEVEL,
        scratch_shapes=[
            pltpu.VMEM((key_rows, width), bf),
            pltpu.VMEM((key_rows, width), bf),
            pltpu.VMEM((heads, HEAD, key_rows), bf),
            pltpu.VMEM((LEVEL * rows, width), bf),
            pltpu.VMEM((LEVEL * rows, width), bf),
            pltpu.VMEM((heads, HEAD, rows), jnp.float32),
            pltpu.SemaphoreType.DMA((n_copies,)),
            pltpu.SemaphoreType.DMA((LEVEL,)),
        ],
        cost_estimate=cost(4 * key_rows * width, 8 * LEVEL * rows * 1024 * width),
        name="attention",
    )(lengths, mask, queries, *q_swapped, own, *swapped, prev_own, prev_rest, ahead)


def gather_out(pieces, rows, width, slab, groups, dtype):
    def kernel(*refs):
        ins, out, sems = refs[:-2], refs[-2], refs[-1]
        j = lax.rem(lax.axis_index("ctx"), LEVEL)
        pairs = []
        for g in range(groups):
            for d in range(LEVEL):
                c = pl.multiple_of((j ^ d) * slab + g * width, 128)
                pairs.append((ins[g * LEVEL + d], out.at[:, pl.ds(c, width)]))
        run_copies(pairs, sems)

    return pl.pallas_call(
        kernel,
        out_shape=jax.ShapeDtypeStruct((rows, LEVEL * slab), dtype),
        in_specs=[ANY] * len(pieces),
        out_specs=VMEM,
        scratch_shapes=[pltpu.SemaphoreType.DMA((len(pieces),))],
        cost_estimate=cost(4 * rows * LEVEL * slab),
        name="gather_out",
    )(*pieces)


def body(queries, key_states, value_states, stretch_lengths, stretch_mask):
    rows, features = queries.shape
    slab = features // LEVEL
    width = slab // GROUPS
    next_blocks = (MAXLEN - 2) // rows + 1
    assert LEVEL * rows >= (WIN + 1) * MAXLEN - 1 and next_blocks <= LEVEL
    others = list(range(1, LEVEL))
    own, swapped, prev_own, prev_rest, ahead = [], [], [], [], []
    for g in range(GROUPS):
        parts = pack_kv(key_states, value_states, g, width, slab, range(LEVEL), "pack_kv")
        own.append(parts[0])
        prev_own.append(shift(parts[0], LEVEL))
        swapped.append([swap(parts[d], d) for d in others])
    q_parts = pack_q(queries, slab)
    q_swapped = [swap(q_parts[d - 1], d) for d in others]
    for g in range(GROUPS):
        fwd, back = pack_z(own[g], swapped[g], next_blocks)
        prev_rest.append(shift(fwd, LEVEL))
        ahead.append(shift(back, -LEVEL))
    pieces = []
    for g in range(GROUPS):
        outs = attention(
            stretch_lengths, stretch_mask, queries, q_swapped, own[g], swapped[g],
            prev_own[g], prev_rest[g], ahead[g], g, width, slab,
        )
        pieces += [outs[0]] + [swap(outs[d], d) for d in others]
    return gather_out(pieces, rows, width, slab, GROUPS, queries.dtype)


def solution(mesh):
    rows = P(("groups", "ctx"), None)
    in_specs = (rows, rows, rows, P("groups"), P("groups", None))
    return jax.shard_map(body, mesh=mesh, in_specs=in_specs, out_specs=rows, check_vma=False)
```

```python
import math

import jax
import jax.numpy as jnp
from jax import lax
from jax.experimental import pallas as pl
from jax.experimental.pallas import tpu as pltpu
from jax.sharding import PartitionSpec as P


HEAD = 128
MAXLEN = 512
WIN = 1
LEVEL = 4
SPLIT = (2, 2, 2)
OTHERS = tuple(range(1, LEVEL))
NEG = -1e30
TILE = 256
HBM = pl.BlockSpec(memory_space=pltpu.HBM)
VMEM = pl.BlockSpec(memory_space=pltpu.VMEM)
SMEM = pl.BlockSpec(memory_space=pltpu.SMEM)


def swap(value, bits):
    return lax.ppermute(value, "ctx", [(i, i ^ bits) for i in range(lax.axis_size("ctx"))])


def swap_levels(value, parity):
    count = lax.axis_size("ctx")
    pairs = []
    for low in range(parity * LEVEL, count - LEVEL, 2 * LEVEL):
        for i in range(low, low + LEVEL):
            pairs += [(i, i + LEVEL), (i + LEVEL, i)]
    return lax.ppermute(value, "ctx", pairs)


def run_copies(pairs, sems):
    copies = [pltpu.make_async_copy(a, b, sems.at[n]) for n, (a, b) in enumerate(pairs)]
    for c in copies:
        c.start()
    for c in copies:
        c.wait()


def cost(nbytes, flops=0):
    return pl.CostEstimate(flops=flops, bytes_accessed=nbytes, transcendentals=0)


def pack_columns(arrays, jobs):
    rows = arrays[0].shape[0]
    totals = [sum(span[3] for span in spans) for _, spans in jobs]

    def kernel(*refs):
        ins, outs, sems = refs[: len(arrays)], refs[len(arrays) : -1], refs[-1]
        j = lax.rem(lax.axis_index("ctx"), LEVEL)
        pairs = []
        for out, (d, spans) in zip(outs, jobs):
            to = 0
            for which, unit, offset, width in spans:
                c = pl.multiple_of((j ^ d) * unit + offset, 128)
                pairs.append((ins[which].at[:, pl.ds(c, width)], out.at[:, pl.ds(to, width)]))
                to += width
        run_copies(pairs, sems)

    return pl.pallas_call(
        kernel,
        out_shape=[jax.ShapeDtypeStruct((rows, total), arrays[0].dtype) for total in totals],
        in_specs=[HBM] * len(arrays),
        out_specs=[VMEM] * len(jobs),
        scratch_shapes=[pltpu.SemaphoreType.DMA((sum(len(spans) for _, spans in jobs),))],
        cost_estimate=cost(4 * rows * sum(totals)),
    )(*arrays)


def pack_z(own, swapped, ahead, offset, width):
    rows = own.shape[0]
    n_fwd = LEVEL - 1

    def kernel(o, *rest):
        outs, sems = rest[LEVEL - 1 : -1], rest[-1]
        pieces = [o.at[:, pl.ds(offset, 2 * width)]]
        pieces += [ref.at[:, pl.ds(0, 2 * width)] for ref in rest[: LEVEL - 1]]
        me = lax.axis_index("ctx")
        j = lax.rem(me, LEVEL)
        odd = lax.rem(me // LEVEL, 2)
        for parity in range(2):
            fwd, back = outs[parity], outs[1 - parity]

            @pl.when(odd == parity)
            def _():
                for d in range(1, LEVEL):
                    pltpu.make_async_copy(pieces[d], fwd.at[d - 1], sems.at[d - 1]).start()
                for b in range(ahead):
                    for d in range(LEVEL):
                        @pl.when((j ^ b) == d)
                        def _():
                            pltpu.make_async_copy(
                                pieces[d], back.at[b], sems.at[n_fwd + b]
                            ).start()
        for n in range(n_fwd + ahead):
            pltpu.make_async_copy(pieces[0], outs[0].at[0], sems.at[n]).wait()

    return pl.pallas_call(
        kernel,
        out_shape=[jax.ShapeDtypeStruct((n_fwd, rows, 2 * width), own.dtype)] * 2,
        in_specs=[HBM] * LEVEL,
        out_specs=[VMEM, VMEM],
        scratch_shapes=[pltpu.SemaphoreType.DMA((n_fwd + ahead,))],
        cost_estimate=cost(8 * rows * width * (n_fwd + ahead)),
        name="pack_z",
    )(own, *swapped)


def lookup_tables(lengths, mask, rows, key_blocks):
    stretches = lengths.shape[0]
    lanes = -(-stretches // HEAD) * HEAD
    key_rows, query_rows = key_blocks * rows, LEVEL * rows

    def kernel(len_ref, mask_ref, bias, onehot, ranges):
        base = (lax.axis_index("ctx") // LEVEL - 1) * query_rows
        lane = lax.broadcasted_iota(jnp.int32, (1, lanes), 1)
        for b in range(LEVEL):
            ranges[b, 0] = jnp.int32(0)
            ranges[b, 1] = jnp.int32(0)

        def scan(a, carry):
            start, before, own, lo, hi = carry
            length = len_ref[a]
            back = jnp.where(mask_ref[a, jnp.maximum(a - 1, 0)] > 0, before, 0)
            end = start + length
            here = lane == a
            for b in range(LEVEL):
                first = (LEVEL + b) * rows
                ranges[b, 0] = jnp.where(start <= first, start - back, ranges[b, 0])
                ranges[b, 1] = jnp.where(start < first + rows, end, ranges[b, 1])
            return (
                end,
                length,
                jnp.where(here, start, own),
                jnp.where(here, start - back, lo),
                jnp.where(here, end, hi),
            )

        zero = jnp.full((1, lanes), -(1 << 30), jnp.int32)
        _, _, own, lo, hi = lax.fori_loop(
            0, stretches, scan, (-base, jnp.int32(0), zero, zero, zero)
        )
        for b in range(LEVEL):
            start = jnp.maximum(ranges[b, 0], 0) // HEAD * HEAD
            tiles = (ranges[b, 1] - start + TILE - 1) // TILE
            ranges[b, 0] = jnp.minimum(start, key_rows - tiles * TILE)
            ranges[b, 1] = tiles

        @pl.loop(0, key_blocks)
        def _(i):
            at = pl.ds(pl.multiple_of(i * rows, rows), rows)
            pos = lax.broadcasted_iota(jnp.int32, (rows, lanes), 0) + i * rows
            inside = (pos >= lo) & (pos < hi)
            bias[at, :] = jnp.where(inside, 0.0, NEG).astype(bias.dtype)

        @pl.loop(0, LEVEL)
        def _(i):
            at = pl.ds(pl.multiple_of(i * rows, rows), rows)
            pos = lax.broadcasted_iota(jnp.int32, (rows, lanes), 0) + (LEVEL + i) * rows
            onehot[at, :] = jnp.where((pos >= own) & (pos < hi), 1.0, 0.0).astype(onehot.dtype)

    bf = jnp.bfloat16
    return pl.pallas_call(
        kernel,
        out_shape=[
            jax.ShapeDtypeStruct((key_rows, lanes), bf),
            jax.ShapeDtypeStruct((query_rows, lanes), bf),
            jax.ShapeDtypeStruct((LEVEL, 2), jnp.int32),
        ],
        in_specs=[SMEM, SMEM],
        out_specs=[VMEM, VMEM, SMEM],
        cost_estimate=cost(2 * (key_rows + query_rows) * lanes),
        name="lookup_tables",
    )(lengths, mask)


def attention(tables, queries, own, swapped, own_far, far, ahead, offset, width, slab):
    rows = queries.shape[0]
    heads = width // HEAD
    key_blocks = 2 * LEVEL + ahead
    key_rows = key_blocks * rows
    lanes = tables[0].shape[1]
    factor = math.log2(math.e) / math.sqrt(HEAD)
    n_copies = 2 + 2 * key_blocks + LEVEL

    def kernel(ranges, bias_hbm, onehot_hbm, q, *rest):
        level, rest = rest[:LEVEL], rest[LEVEL:]
        own_sides, sides, rest = rest[:2], rest[2:4], rest[4:]
        outs, scratch = rest[:LEVEL], rest[LEVEL:]
        ks, vs, vt, qs, os, acc, bias, onehot, sems, out_sems = scratch
        me = lax.axis_index("ctx")
        j = lax.rem(me, LEVEL)
        odd = lax.rem(me // LEVEL, 2)

        def kv(src, block, off=0):
            at = pl.ds(pl.multiple_of(block * rows, rows), rows)
            return [
                (src.at[:, pl.ds(off, width)], ks.at[at, :]),
                (src.at[:, pl.ds(off + width, width)], vs.at[at, :]),
            ]

        pairs = [(bias_hbm, bias), (onehot_hbm, onehot)]
        for d in range(LEVEL):
            pairs += kv(level[d], LEVEL + (j ^ d), 2 * offset if d == 0 else 0)
            at = pl.ds(pl.multiple_of((j ^ d) * rows, rows), rows)
            if d == 0:
                c = pl.multiple_of(j * slab + offset, HEAD)
                pairs.append((q.at[:, pl.ds(c, width)], qs.at[at, :]))
            else:
                pairs.append((level[d].at[:, pl.ds(2 * width, width)], qs.at[at, :]))
        near = len(pairs)

        def side_pairs(parity):
            behind, front = 1 - parity, parity
            out = kv(own_sides[behind], j, 2 * offset)
            for d in range(1, LEVEL):
                out += kv(sides[behind].at[d - 1], j ^ d)
            for b in range(ahead):
                out += kv(sides[front].at[b], 2 * LEVEL + b)
            return out

        copies = [pltpu.make_async_copy(a, b, sems.at[n]) for n, (a, b) in enumerate(pairs)]
        for c in copies:
            c.start()
        for parity in range(2):
            @pl.when(odd == parity)
            def _():
                for n, (a, b) in enumerate(side_pairs(parity)):
                    pltpu.make_async_copy(a, b, sems.at[near + n]).start()
        copies += [
            pltpu.make_async_copy(a, b, sems.at[near + n])
            for n, (a, b) in enumerate(side_pairs(0))
        ]
        for c in copies:
            c.wait()
        for h in range(heads):
            vt[h, HEAD:, :] = jnp.ones_like(vt[h, HEAD:, :])

        @pl.loop(0, key_rows // TILE)
        def _(i):
            at = pl.ds(pl.multiple_of(i * TILE, TILE), TILE)
            for h in range(heads):
                vt[h, :HEAD, at] = vs[at, h * HEAD : (h + 1) * HEAD].T

        @pl.loop(0, LEVEL)
        def _(b):
            at = pl.ds(pl.multiple_of(b * rows, rows), rows)
            start, tiles = ranges[b, 0], ranges[b, 1]
            for h in range(heads):
                acc[h] = jnp.zeros_like(acc[h])
            q_ext = [
                jnp.concatenate([qs[at, h * HEAD : (h + 1) * HEAD], onehot[at, :]], axis=1)
                for h in range(heads)
            ]

            def step(t, tops):
                k_at = pl.ds(pl.multiple_of(start + t * TILE, HEAD), TILE)
                scores = [
                    lax.dot_general(
                        jnp.concatenate(
                            [ks[k_at, h * HEAD : (h + 1) * HEAD], bias[k_at, :]], axis=1
                        ),
                        q_ext[h],
                        (((1,), (1,)), ((), ())),
                        preferred_element_type=jnp.float32,
                    )
                    for h in range(heads)
                ]
                new = []
                for h in range(heads):
                    s, top = scores[h], tops[h]
                    top_new = jnp.maximum(top, jnp.max(s, axis=0, keepdims=True))
                    p = jnp.exp2((s - top_new) * factor).astype(jnp.bfloat16)
                    alpha = jnp.exp2((top - top_new) * factor)
                    acc[h] = acc[h] * alpha + jnp.dot(
                        vt[h, :, k_at], p, preferred_element_type=jnp.float32
                    )
                    new.append(top_new)
                return tuple(new)

            low = jnp.full((1, rows), 2 * NEG, jnp.float32)
            lax.fori_loop(0, tiles, step, (low,) * heads)
            for h in range(heads):
                normed = acc[h, :HEAD, :] / acc[h, HEAD : HEAD + 1, :]
                os[at, h * HEAD : (h + 1) * HEAD] = normed.T.astype(jnp.bfloat16)

        run_copies(
            [
                (os.at[pl.ds(pl.multiple_of((j ^ d) * rows, rows), rows), :], outs[d])
                for d in range(LEVEL)
            ],
            out_sems,
        )

    bf = jnp.bfloat16
    bias, onehot, ranges = tables
    return pl.pallas_call(
        kernel,
        out_shape=[jax.ShapeDtypeStruct((rows, width), bf)] * LEVEL,
        in_specs=[SMEM] + [HBM] * (LEVEL + 7),
        out_specs=[HBM] * LEVEL,
        scratch_shapes=[
            pltpu.VMEM((key_rows, width), bf),
            pltpu.VMEM((key_rows, width), bf),
            pltpu.VMEM((heads, HEAD + 16, key_rows), bf),
            pltpu.VMEM((LEVEL * rows, width), bf),
            pltpu.VMEM((LEVEL * rows, width), bf),
            pltpu.VMEM((heads, HEAD + 16, rows), jnp.float32),
            pltpu.VMEM((key_rows, lanes), bf),
            pltpu.VMEM((LEVEL * rows, lanes), bf),
            pltpu.SemaphoreType.DMA((n_copies,)),
            pltpu.SemaphoreType.DMA((LEVEL,)),
        ],
        cost_estimate=cost(4 * key_rows * width, 8 * LEVEL * rows * 1024 * width),
        name="attention",
    )(ranges, bias, onehot, queries, own, *swapped, *own_far, *far)


def gather_out(pieces, rows, slab, dtype):
    def kernel(*refs):
        ins, out, sems = refs[:-2], refs[-2], refs[-1]
        j = lax.rem(lax.axis_index("ctx"), LEVEL)
        pairs, offset = [], 0
        for g, heads in enumerate(SPLIT):
            width = heads * HEAD
            for d in range(LEVEL):
                c = pl.multiple_of((j ^ d) * slab + offset, HEAD)
                pairs.append((ins[g * LEVEL + d], out.at[:, pl.ds(c, width)]))
            offset += width
        run_copies(pairs, sems)

    return pl.pallas_call(
        kernel,
        out_shape=jax.ShapeDtypeStruct((rows, LEVEL * slab), dtype),
        in_specs=[HBM] * len(pieces),
        out_specs=VMEM,
        scratch_shapes=[pltpu.SemaphoreType.DMA((len(pieces),))],
        cost_estimate=cost(4 * rows * LEVEL * slab),
        name="gather_out",
    )(*pieces)


def attend(queries, key_states, value_states, stretch_lengths, stretch_mask):
    rows, features = queries.shape
    slab = features // LEVEL
    ahead = (MAXLEN - 2) // rows + 1
    assert LEVEL * rows >= (WIN + 1) * MAXLEN - 1 and ahead < LEVEL
    assert sum(SPLIT) * HEAD == slab
    widths = [heads * HEAD for heads in SPLIT]
    offsets = [sum(widths[:g]) for g in range(len(widths))]
    groups = range(len(SPLIT))
    arrays = (key_states, value_states, queries)
    tables = lookup_tables(stretch_lengths, stretch_mask, rows, 2 * LEVEL + ahead)
    slabs = [[(i, slab, offsets[g], widths[g]) for i in range(3)] for g in groups]
    own_spans = [span for spans in slabs for span in spans[:2]]
    jobs = [(d, slabs[0]) for d in OTHERS] + [(0, own_spans)]
    *parts, own = pack_columns(arrays, jobs)
    jobs = [(d, slabs[g]) for g in groups[1:] for d in OTHERS]
    parts += pack_columns(arrays, jobs)
    swapped, far = [], []
    for g in groups:
        mine = parts[g * len(OTHERS) : (g + 1) * len(OTHERS)]
        swapped.append([swap(x, d) for x, d in zip(mine, OTHERS)])
    own_far = [swap_levels(own, p) for p in range(2)]
    for g in groups:
        sides = pack_z(own, swapped[g], ahead, 2 * offsets[g], widths[g])
        far.append([swap_levels(x, p) for p, x in enumerate(sides)])
    pieces = []
    for g in groups:
        outs = attention(
            tables, queries, own, swapped[g], own_far, far[g], ahead,
            offsets[g], widths[g], slab,
        )
        pieces += [outs[0]]
        pieces += [swap(outs[d], d) for d in OTHERS]
    return gather_out(pieces, rows, slab, queries.dtype)


def solution(mesh):
    rows = P(("groups", "ctx"), None)
    in_specs = (rows, rows, rows, P("groups"), P("groups", None))
    return jax.shard_map(attend, mesh=mesh, in_specs=in_specs, out_specs=rows, check_vma=False)
```

```python
import math

import jax
import jax.numpy as jnp
from jax import lax
from jax.experimental import pallas as pl
from jax.experimental.pallas import tpu as pltpu
from jax.sharding import PartitionSpec as P


HEAD = 128
MAXLEN = 512
WIN = 1
LEVEL = 4
SPLIT = (2, 2, 2)
OTHERS = tuple(range(1, LEVEL))
NEG = -1e30
TILE = 256
SIZES = (2, 3, 4, 5, 6, 8)
HBM = pl.BlockSpec(memory_space=pl.ANY)
VMEM = pl.BlockSpec(memory_space=pltpu.VMEM)
SMEM = pl.BlockSpec(memory_space=pltpu.SMEM)


def swap(value, bits):
    return lax.ppermute(value, "ctx", [(i, i ^ bits) for i in range(lax.axis_size("ctx"))])


def swap_levels(value, parity):
    count = lax.axis_size("ctx")
    pairs = []
    for low in range(parity * LEVEL, count - LEVEL, 2 * LEVEL):
        for i in range(low, low + LEVEL):
            pairs += [(i, i + LEVEL), (i + LEVEL, i)]
    return lax.ppermute(value, "ctx", pairs)


def run_copies(pairs, sems):
    copies = [pltpu.make_async_copy(a, b, sems.at[n]) for n, (a, b) in enumerate(pairs)]
    for c in copies:
        c.start()
    for c in copies:
        c.wait()


def cost(nbytes, flops=0):
    return pl.CostEstimate(flops=flops, bytes_accessed=nbytes, transcendentals=0)


def pack_columns(arrays, jobs):
    rows = arrays[0].shape[0]
    totals = [sum(span[3] for span in spans) for _, spans in jobs]

    def kernel(*refs):
        ins, outs, sems = refs[: len(arrays)], refs[len(arrays) : -1], refs[-1]
        j = lax.rem(lax.axis_index("ctx"), LEVEL)
        pairs = []
        for out, (d, spans) in zip(outs, jobs):
            to = 0
            for which, unit, offset, width in spans:
                c = pl.multiple_of((j ^ d) * unit + offset, 128)
                pairs.append((ins[which].at[:, pl.ds(c, width)], out.at[:, pl.ds(to, width)]))
                to += width
        run_copies(pairs, sems)

    return pl.pallas_call(
        kernel,
        out_shape=[jax.ShapeDtypeStruct((rows, total), arrays[0].dtype) for total in totals],
        in_specs=[HBM] * len(arrays),
        out_specs=[VMEM] * len(jobs),
        scratch_shapes=[pltpu.SemaphoreType.DMA((sum(len(spans) for _, spans in jobs),))],
        cost_estimate=cost(4 * rows * sum(totals)),
    )(*arrays)


def pack_z(own, swapped, ahead, offset, width):
    rows = own.shape[0]
    n_fwd = LEVEL - 1

    def kernel(o, *rest):
        outs, sems = rest[LEVEL - 1 : -1], rest[-1]
        pieces = [o.at[:, pl.ds(offset, 2 * width)]]
        pieces += [ref.at[:, pl.ds(0, 2 * width)] for ref in rest[: LEVEL - 1]]
        me = lax.axis_index("ctx")
        j = lax.rem(me, LEVEL)
        odd = lax.rem(me // LEVEL, 2)
        for parity in range(2):
            fwd, back = outs[parity], outs[1 - parity]

            @pl.when(odd == parity)
            def _():
                for d in range(1, LEVEL):
                    pltpu.make_async_copy(pieces[d], fwd.at[d - 1], sems.at[d - 1]).start()
                for b in range(ahead):
                    for d in range(LEVEL):
                        @pl.when((j ^ b) == d)
                        def _():
                            pltpu.make_async_copy(
                                pieces[d], back.at[b], sems.at[n_fwd + b]
                            ).start()
        for n in range(n_fwd + ahead):
            pltpu.make_async_copy(pieces[0], outs[0].at[0], sems.at[n]).wait()

    return pl.pallas_call(
        kernel,
        out_shape=[jax.ShapeDtypeStruct((n_fwd, rows, 2 * width), own.dtype)] * 2,
        in_specs=[HBM] * LEVEL,
        out_specs=[VMEM, VMEM],
        scratch_shapes=[pltpu.SemaphoreType.DMA((n_fwd + ahead,))],
        cost_estimate=cost(8 * rows * width * (n_fwd + ahead)),
        name="pack_z",
    )(own, *swapped)


def lookup_tables(lengths, mask, rows, key_blocks):
    stretches = lengths.shape[0]
    lanes = -(-stretches // HEAD) * HEAD
    key_rows, query_rows = key_blocks * rows, LEVEL * rows

    def kernel(len_ref, mask_ref, bias, onehot, ranges):
        base = (lax.axis_index("ctx") // LEVEL - 1) * query_rows
        lane = lax.broadcasted_iota(jnp.int32, (1, lanes), 1)
        for b in range(LEVEL):
            ranges[b, 0] = jnp.int32(0)
            ranges[b, 1] = jnp.int32(0)

        def scan(a, carry):
            start, before, own, lo, hi = carry
            length = len_ref[a]
            back = jnp.where(mask_ref[a, jnp.maximum(a - 1, 0)] > 0, before, 0)
            end = start + length
            here = lane == a
            for b in range(LEVEL):
                first = (LEVEL + b) * rows
                ranges[b, 0] = jnp.where(start <= first, start - back, ranges[b, 0])
                ranges[b, 1] = jnp.where(start < first + rows, end, ranges[b, 1])
            return (
                end,
                length,
                jnp.where(here, start, own),
                jnp.where(here, start - back, lo),
                jnp.where(here, end, hi),
            )

        zero = jnp.full((1, lanes), -(1 << 30), jnp.int32)
        _, _, own, lo, hi = lax.fori_loop(
            0, stretches, scan, (-base, jnp.int32(0), zero, zero, zero)
        )
        for b in range(LEVEL):
            start = jnp.maximum(ranges[b, 0], 0) // HEAD * HEAD
            tiles = jnp.int32(SIZES[-1])
            for size in SIZES[-2::-1]:
                tiles = jnp.where(ranges[b, 1] - start <= size * TILE, size, tiles)
            ranges[b, 0] = jnp.minimum(start, key_rows - tiles * TILE)
            ranges[b, 1] = tiles

        @pl.loop(0, key_blocks)
        def _(i):
            at = pl.ds(pl.multiple_of(i * rows, rows), rows)
            pos = lax.broadcasted_iota(jnp.int32, (rows, lanes), 0) + i * rows
            inside = (pos >= lo) & (pos < hi)
            bias[at, :] = jnp.where(inside, 0.0, NEG).astype(bias.dtype)

        @pl.loop(0, LEVEL)
        def _(i):
            at = pl.ds(pl.multiple_of(i * rows, rows), rows)
            pos = lax.broadcasted_iota(jnp.int32, (rows, lanes), 0) + (LEVEL + i) * rows
            onehot[at, :] = jnp.where((pos >= own) & (pos < hi), 1.0, 0.0).astype(onehot.dtype)

    bf = jnp.bfloat16
    return pl.pallas_call(
        kernel,
        out_shape=[
            jax.ShapeDtypeStruct((key_rows, lanes), bf),
            jax.ShapeDtypeStruct((query_rows, lanes), bf),
            jax.ShapeDtypeStruct((LEVEL, 2), jnp.int32),
        ],
        in_specs=[SMEM, SMEM],
        out_specs=[VMEM, VMEM, SMEM],
        cost_estimate=cost(2 * (key_rows + query_rows) * lanes),
        name="lookup_tables",
    )(lengths, mask)


def attention(tables, queries, own, swapped, own_far, far, ahead, offset, width, slab):
    rows = queries.shape[0]
    heads = width // HEAD
    key_blocks = 2 * LEVEL + ahead
    key_rows = key_blocks * rows
    lanes = tables[0].shape[1]
    factor = math.log2(math.e) / math.sqrt(HEAD)
    n_copies = 2 + 2 * key_blocks + LEVEL

    def kernel(ranges, bias_hbm, onehot_hbm, q, *rest):
        level, rest = rest[:LEVEL], rest[LEVEL:]
        own_sides, sides, rest = rest[:2], rest[2:4], rest[4:]
        outs, scratch = rest[:LEVEL], rest[LEVEL:]
        ks, vs, vt, qs, os, bias, onehot, sems, out_sems = scratch
        me = lax.axis_index("ctx")
        j = lax.rem(me, LEVEL)
        odd = lax.rem(me // LEVEL, 2)

        def kv(src, block, off=0):
            at = pl.ds(pl.multiple_of(block * rows, rows), rows)
            return [
                (src.at[:, pl.ds(off, width)], ks.at[at, :]),
                (src.at[:, pl.ds(off + width, width)], vs.at[at, :]),
            ]

        pairs = [(bias_hbm, bias), (onehot_hbm, onehot)]
        for d in range(LEVEL):
            pairs += kv(level[d], LEVEL + (j ^ d), 2 * offset if d == 0 else 0)
            at = pl.ds(pl.multiple_of((j ^ d) * rows, rows), rows)
            if d == 0:
                c = pl.multiple_of(j * slab + offset, HEAD)
                pairs.append((q.at[:, pl.ds(c, width)], qs.at[at, :]))
            else:
                pairs.append((level[d].at[:, pl.ds(2 * width, width)], qs.at[at, :]))
        near = len(pairs)

        def side_pairs(parity):
            behind, front = 1 - parity, parity
            out = kv(own_sides[behind], j, 2 * offset)
            for d in range(1, LEVEL):
                out += kv(sides[behind].at[d - 1], j ^ d)
            for b in range(ahead):
                out += kv(sides[front].at[b], 2 * LEVEL + b)
            return out

        copies = [pltpu.make_async_copy(a, b, sems.at[n]) for n, (a, b) in enumerate(pairs)]
        for c in copies:
            c.start()
        for parity in range(2):
            @pl.when(odd == parity)
            def _():
                for n, (a, b) in enumerate(side_pairs(parity)):
                    pltpu.make_async_copy(a, b, sems.at[near + n]).start()
        copies += [
            pltpu.make_async_copy(a, b, sems.at[near + n])
            for n, (a, b) in enumerate(side_pairs(0))
        ]
        for c in copies:
            c.wait()
        for h in range(heads):
            vt[h, HEAD:, :] = jnp.ones_like(vt[h, HEAD:, :])

        @pl.loop(0, key_rows // TILE)
        def _(i):
            at = pl.ds(pl.multiple_of(i * TILE, TILE), TILE)
            for h in range(heads):
                vt[h, :HEAD, at] = vs[at, h * HEAD : (h + 1) * HEAD].T

        @pl.loop(0, LEVEL)
        def _(b):
            at = pl.ds(pl.multiple_of(b * rows, rows), rows)
            start = pl.multiple_of(ranges[b, 0], HEAD)
            for size in SIZES:
                @pl.when(ranges[b, 1] == size)
                def _():
                    k_at = pl.ds(start, size * TILE)
                    scores = [
                        lax.dot_general(
                            jnp.concatenate(
                                [ks[k_at, h * HEAD : (h + 1) * HEAD], bias[k_at, :]], axis=1
                            ),
                            jnp.concatenate(
                                [qs[at, h * HEAD : (h + 1) * HEAD], onehot[at, :]], axis=1
                            ),
                            (((1,), (1,)), ((), ())),
                            preferred_element_type=jnp.float32,
                        )
                        for h in range(heads)
                    ]
                    for h, s in enumerate(scores):
                        top = jnp.max(s, axis=0, keepdims=True)
                        p = jnp.exp2((s - top) * factor).astype(jnp.bfloat16)
                        both = jnp.dot(vt[h, :, k_at], p, preferred_element_type=jnp.float32)
                        normed = both[:HEAD] / both[HEAD : HEAD + 1]
                        os[at, h * HEAD : (h + 1) * HEAD] = normed.T.astype(jnp.bfloat16)

        run_copies(
            [
                (os.at[pl.ds(pl.multiple_of((j ^ d) * rows, rows), rows), :], outs[d])
                for d in range(LEVEL)
            ],
            out_sems,
        )

    bf = jnp.bfloat16
    bias, onehot, ranges = tables
    return pl.pallas_call(
        kernel,
        out_shape=[jax.ShapeDtypeStruct((rows, width), bf)] * LEVEL,
        in_specs=[SMEM] + [HBM] * (LEVEL + 7),
        out_specs=[HBM] * LEVEL,
        scratch_shapes=[
            pltpu.VMEM((key_rows, width), bf),
            pltpu.VMEM((key_rows, width), bf),
            pltpu.VMEM((heads, HEAD + 16, key_rows), bf),
            pltpu.VMEM((LEVEL * rows, width), bf),
            pltpu.VMEM((LEVEL * rows, width), bf),
            pltpu.VMEM((key_rows, lanes), bf),
            pltpu.VMEM((LEVEL * rows, lanes), bf),
            pltpu.SemaphoreType.DMA((n_copies,)),
            pltpu.SemaphoreType.DMA((LEVEL,)),
        ],
        cost_estimate=cost(4 * key_rows * width, 8 * LEVEL * rows * 1024 * width),
        name="attention",
    )(ranges, bias, onehot, queries, own, *swapped, *own_far, *far)


def gather_out(pieces, rows, slab, dtype):
    def kernel(*refs):
        ins, out, sems = refs[:-2], refs[-2], refs[-1]
        j = lax.rem(lax.axis_index("ctx"), LEVEL)
        pairs, offset = [], 0
        for g, heads in enumerate(SPLIT):
            width = heads * HEAD
            for d in range(LEVEL):
                c = pl.multiple_of((j ^ d) * slab + offset, HEAD)
                pairs.append((ins[g * LEVEL + d], out.at[:, pl.ds(c, width)]))
            offset += width
        run_copies(pairs, sems)

    return pl.pallas_call(
        kernel,
        out_shape=jax.ShapeDtypeStruct((rows, LEVEL * slab), dtype),
        in_specs=[HBM] * len(pieces),
        out_specs=VMEM,
        scratch_shapes=[pltpu.SemaphoreType.DMA((len(pieces),))],
        cost_estimate=cost(4 * rows * LEVEL * slab),
        name="gather_out",
    )(*pieces)


def attend(queries, key_states, value_states, stretch_lengths, stretch_mask):
    rows, features = queries.shape
    slab = features // LEVEL
    ahead = (MAXLEN - 2) // rows + 1
    assert LEVEL * rows >= (WIN + 1) * MAXLEN - 1 and ahead < LEVEL
    assert sum(SPLIT) * HEAD == slab
    assert (WIN + 2) * MAXLEN + rows + HEAD <= SIZES[-1] * TILE + 4
    widths = [heads * HEAD for heads in SPLIT]
    offsets = [sum(widths[:g]) for g in range(len(widths))]
    groups = range(len(SPLIT))
    arrays = (key_states, value_states, queries)
    tables = lookup_tables(stretch_lengths, stretch_mask, rows, 2 * LEVEL + ahead)
    slabs = [[(i, slab, offsets[g], widths[g]) for i in range(3)] for g in groups]
    own_spans = [span for spans in slabs for span in spans[:2]]
    jobs = [(d, slabs[0]) for d in OTHERS] + [(0, own_spans)]
    *parts, own = pack_columns(arrays, jobs)
    jobs = [(d, slabs[g]) for g in groups[1:] for d in OTHERS]
    parts += pack_columns(arrays, jobs)
    swapped, far = [], []
    for g in groups:
        mine = parts[g * len(OTHERS) : (g + 1) * len(OTHERS)]
        swapped.append([swap(x, d) for x, d in zip(mine, OTHERS)])
    own_far = [swap_levels(own, p) for p in range(2)]
    for g in groups:
        sides = pack_z(own, swapped[g], ahead, 2 * offsets[g], widths[g])
        far.append([swap_levels(x, p) for p, x in enumerate(sides)])
    pieces = []
    for g in groups:
        outs = attention(
            tables, queries, own, swapped[g], own_far, far[g], ahead,
            offsets[g], widths[g], slab,
        )
        pieces += [outs[0]]
        pieces += [swap(outs[d], d) for d in OTHERS]
    return gather_out(pieces, rows, slab, queries.dtype)


def solution(mesh):
    rows = P(("groups", "ctx"), None)
    in_specs = (rows, rows, rows, P("groups"), P("groups", None))
    return jax.shard_map(attend, mesh=mesh, in_specs=in_specs, out_specs=rows, check_vma=False)
```

```python
import math

import jax
import jax.numpy as jnp
from jax import lax
from jax.experimental import pallas as pl
from jax.experimental.pallas import tpu as pltpu
from jax.sharding import PartitionSpec as P


HEAD = 128
MAXLEN = 512
WIN = 1
LEVEL = 4
SPLIT = (2, 2, 2)
OTHERS = tuple(range(1, LEVEL))
NEG = -1e30
TILE = 256
SIZES = (2, 3, 4, 5, 6, 8)
HBM = pl.BlockSpec(memory_space=pl.ANY)
VMEM = pl.BlockSpec(memory_space=pltpu.VMEM)
SMEM = pl.BlockSpec(memory_space=pltpu.SMEM)


def swap(value, bits):
    return lax.ppermute(value, "ctx", [(i, i ^ bits) for i in range(lax.axis_size("ctx"))])


def swap_levels(value, parity):
    count = lax.axis_size("ctx")
    pairs = {i: i ^ 1 for i in range(count)}
    for low in range(parity * LEVEL, count - LEVEL, 2 * LEVEL):
        for i in range(low, low + LEVEL):
            pairs[i], pairs[i + LEVEL] = i + LEVEL, i
    return lax.ppermute(value, "ctx", sorted(pairs.items()))


def run_copies(pairs, sems):
    copies = [pltpu.make_async_copy(a, b, sems.at[n]) for n, (a, b) in enumerate(pairs)]
    for c in copies:
        c.start()
    for c in copies:
        c.wait()


def cost(nbytes, flops=0):
    return pl.CostEstimate(flops=flops, bytes_accessed=nbytes, transcendentals=0)


def pack_columns(arrays, jobs):
    rows = arrays[0].shape[0]
    totals = [sum(span[3] for span in spans) for _, spans in jobs]

    def kernel(*refs):
        ins, outs, sems = refs[: len(arrays)], refs[len(arrays) : -1], refs[-1]
        j = lax.rem(lax.axis_index("ctx"), LEVEL)
        pairs = []
        for out, (d, spans) in zip(outs, jobs):
            to = 0
            for which, unit, offset, width in spans:
                c = pl.multiple_of((j ^ d) * unit + offset, 128)
                pairs.append((ins[which].at[:, pl.ds(c, width)], out.at[:, pl.ds(to, width)]))
                to += width
        run_copies(pairs, sems)

    return pl.pallas_call(
        kernel,
        out_shape=[jax.ShapeDtypeStruct((rows, total), arrays[0].dtype) for total in totals],
        in_specs=[HBM] * len(arrays),
        out_specs=[VMEM] * len(jobs),
        scratch_shapes=[pltpu.SemaphoreType.DMA((sum(len(spans) for _, spans in jobs),))],
        cost_estimate=cost(4 * rows * sum(totals)),
    )(*arrays)


def pack_z(own, swapped, ahead, offset, width):
    rows = own.shape[0]
    n_fwd = LEVEL - 1

    def kernel(o, *rest):
        outs, sems = rest[LEVEL - 1 : -1], rest[-1]
        pieces = [o.at[:, pl.ds(offset, 2 * width)]]
        pieces += [ref.at[:, pl.ds(0, 2 * width)] for ref in rest[: LEVEL - 1]]
        me = lax.axis_index("ctx")
        j = lax.rem(me, LEVEL)
        odd = lax.rem(me // LEVEL, 2)
        for parity in range(2):
            fwd, back = outs[parity], outs[1 - parity]

            @pl.when(odd == parity)
            def _():
                for d in range(1, LEVEL):
                    pltpu.make_async_copy(pieces[d], fwd.at[d - 1], sems.at[d - 1]).start()
                for b in range(ahead):
                    for d in range(LEVEL):
                        @pl.when((j ^ b) == d)
                        def _():
                            pltpu.make_async_copy(
                                pieces[d], back.at[b], sems.at[n_fwd + b]
                            ).start()
        for n in range(n_fwd + ahead):
            pltpu.make_async_copy(pieces[0], outs[0].at[0], sems.at[n]).wait()

    return pl.pallas_call(
        kernel,
        out_shape=[jax.ShapeDtypeStruct((n_fwd, rows, 2 * width), own.dtype)] * 2,
        in_specs=[HBM] * LEVEL,
        out_specs=[VMEM, VMEM],
        scratch_shapes=[pltpu.SemaphoreType.DMA((n_fwd + ahead,))],
        cost_estimate=cost(8 * rows * width * (n_fwd + ahead)),
        name="pack_z",
    )(own, *swapped)


def lookup_tables(lengths, mask, rows, key_blocks):
    stretches = lengths.shape[0]
    lanes = -(-stretches // HEAD) * HEAD
    key_rows, query_rows = key_blocks * rows, LEVEL * rows

    def kernel(len_ref, mask_ref, bias, onehot, ranges):
        base = (lax.axis_index("ctx") // LEVEL - 1) * query_rows
        lane = lax.broadcasted_iota(jnp.int32, (1, lanes), 1)
        for b in range(LEVEL):
            ranges[b, 0] = jnp.int32(0)
            ranges[b, 1] = jnp.int32(0)

        def scan(a, carry):
            start, before, own, lo, hi = carry
            length = len_ref[a]
            back = jnp.where(mask_ref[a, jnp.maximum(a - 1, 0)] > 0, before, 0)
            end = start + length
            here = lane == a
            for b in range(LEVEL):
                first = (LEVEL + b) * rows
                ranges[b, 0] = jnp.where(start <= first, start - back, ranges[b, 0])
                ranges[b, 1] = jnp.where(start < first + rows, end, ranges[b, 1])
            return (
                end,
                length,
                jnp.where(here, start, own),
                jnp.where(here, start - back, lo),
                jnp.where(here, end, hi),
            )

        zero = jnp.full((1, lanes), -(1 << 30), jnp.int32)
        _, _, own, lo, hi = lax.fori_loop(
            0, stretches, scan, (-base, jnp.int32(0), zero, zero, zero)
        )
        for b in range(LEVEL):
            start = jnp.maximum(ranges[b, 0], 0) // HEAD * HEAD
            tiles = jnp.int32(SIZES[-1])
            for size in SIZES[-2::-1]:
                tiles = jnp.where(ranges[b, 1] - start <= size * TILE, size, tiles)
            ranges[b, 0] = jnp.minimum(start, key_rows - tiles * TILE)
            ranges[b, 1] = tiles
        low, high = jnp.int32(key_rows), jnp.int32(0)
        for b in range(LEVEL):
            low = jnp.minimum(low, ranges[b, 0])
            high = jnp.maximum(high, ranges[b, 0] + ranges[b, 1] * TILE)
        ranges[LEVEL, 0] = low // rows
        ranges[LEVEL, 1] = (high + rows - 1) // rows

        @pl.loop(0, key_blocks)
        def _(i):
            at = pl.ds(pl.multiple_of(i * rows, rows), rows)
            pos = lax.broadcasted_iota(jnp.int32, (rows, lanes), 0) + i * rows
            inside = (pos >= lo) & (pos < hi)
            bias[at, :] = jnp.where(inside, 0.0, NEG).astype(bias.dtype)

        @pl.loop(0, LEVEL)
        def _(i):
            at = pl.ds(pl.multiple_of(i * rows, rows), rows)
            pos = lax.broadcasted_iota(jnp.int32, (rows, lanes), 0) + (LEVEL + i) * rows
            onehot[at, :] = jnp.where((pos >= own) & (pos < hi), 1.0, 0.0).astype(onehot.dtype)

    bf = jnp.bfloat16
    return pl.pallas_call(
        kernel,
        out_shape=[
            jax.ShapeDtypeStruct((key_rows, lanes), bf),
            jax.ShapeDtypeStruct((query_rows, lanes), bf),
            jax.ShapeDtypeStruct((LEVEL + 1, 2), jnp.int32),
        ],
        in_specs=[SMEM, SMEM],
        out_specs=[VMEM, VMEM, SMEM],
        cost_estimate=cost(2 * (key_rows + query_rows) * lanes),
        name="lookup_tables",
    )(lengths, mask)


def attention(
    tables, queries, own, swapped, q_swapped, own_far, far, ahead, offset, width, q_offset, slab
):
    rows = queries.shape[0]
    heads = width // HEAD
    key_blocks = 2 * LEVEL + ahead
    key_rows = key_blocks * rows
    lanes = tables[0].shape[1]
    factor = math.log2(math.e) / math.sqrt(HEAD)
    n_copies = 2 * key_blocks + 2 + LEVEL

    def kernel(ranges, bias_hbm, onehot_hbm, q, *rest):
        level, rest = rest[:LEVEL], rest[LEVEL:]
        asked, rest = rest[: LEVEL - 1], rest[LEVEL - 1 :]
        own_sides, sides, rest = rest[:2], rest[2:4], rest[4:]
        outs, scratch = rest[:LEVEL], rest[LEVEL:]
        ks, vs, vt, qs, os, bias, onehot, sems, out_sems = scratch
        me = lax.axis_index("ctx")
        j = lax.rem(me, LEVEL)
        odd = lax.rem(me // LEVEL, 2)

        def kv(src, block, off=0):
            at = pl.ds(pl.multiple_of(block * rows, rows), rows)
            value = pltpu.make_async_copy(
                src.at[:, pl.ds(off + width, width)], vs.at[at, :], sems.at[block]
            )
            key = pltpu.make_async_copy(
                src.at[:, pl.ds(off, width)], ks.at[at, :], sems.at[key_blocks + block]
            )
            return [value, key]

        def level_copies():
            copies = []
            for d in range(LEVEL):
                copies += kv(level[d], LEVEL + (j ^ d), 2 * offset if d == 0 else 0)
            return copies

        rest_pairs = [(bias_hbm, bias), (onehot_hbm, onehot)]
        for d in range(LEVEL):
            at = pl.ds(pl.multiple_of((j ^ d) * rows, rows), rows)
            if d == 0:
                c = pl.multiple_of(j * slab + offset, HEAD)
                rest_pairs.append((q.at[:, pl.ds(c, width)], qs.at[at, :]))
            else:
                rest_pairs.append((asked[d - 1].at[:, pl.ds(q_offset, width)], qs.at[at, :]))

        def side_copies(parity):
            behind, front = 1 - parity, parity
            out = kv(own_sides[behind], j, 2 * offset)
            for d in range(1, LEVEL):
                out += kv(sides[behind].at[d - 1], j ^ d)
            for b in range(ahead):
                out += kv(sides[front].at[b], 2 * LEVEL + b)
            return out

        near = level_copies()
        rest = [
            pltpu.make_async_copy(a, b, sems.at[2 * key_blocks + n])
            for n, (a, b) in enumerate(rest_pairs)
        ]
        for part in range(2):
            for c in near[part::2]:
                c.start()
            for parity in range(2):
                @pl.when(odd == parity)
                def _():
                    for c in side_copies(parity)[part::2]:
                        c.start()
        for c in rest:
            c.start()
        for h in range(heads):
            vt[h, HEAD:, :] = jnp.ones_like(vt[h, HEAD:, :])

        @pl.loop(0, key_blocks)
        def _(i):
            at = pl.ds(pl.multiple_of(i * rows, rows), rows)
            pltpu.make_async_copy(ks.at[at, :], vs.at[at, :], sems.at[i]).wait()

            @pl.when((i >= ranges[LEVEL, 0]) & (i < ranges[LEVEL, 1]))
            def _():
                for h in range(heads):
                    vt[h, :HEAD, at] = vs[at, h * HEAD : (h + 1) * HEAD].T

        @pl.loop(0, key_blocks)
        def _(i):
            at = pl.ds(pl.multiple_of(i * rows, rows), rows)
            pltpu.make_async_copy(vs.at[at, :], ks.at[at, :], sems.at[key_blocks + i]).wait()

        for c in rest:
            c.wait()

        @pl.loop(0, LEVEL)
        def _(b):
            at = pl.ds(pl.multiple_of(b * rows, rows), rows)
            start = pl.multiple_of(ranges[b, 0], HEAD)
            for size in SIZES:
                @pl.when(ranges[b, 1] == size)
                def _():
                    k_at = pl.ds(start, size * TILE)
                    scores = [
                        lax.dot_general(
                            jnp.concatenate(
                                [ks[k_at, h * HEAD : (h + 1) * HEAD], bias[k_at, :]], axis=1
                            ),
                            jnp.concatenate(
                                [qs[at, h * HEAD : (h + 1) * HEAD], onehot[at, :]], axis=1
                            ),
                            (((1,), (1,)), ((), ())),
                            preferred_element_type=jnp.float32,
                        )
                        for h in range(heads)
                    ]
                    for h, s in enumerate(scores):
                        top = jnp.max(s, axis=0, keepdims=True)
                        p = jnp.exp2((s - top) * factor).astype(jnp.bfloat16)
                        both = jnp.dot(vt[h, :, k_at], p, preferred_element_type=jnp.float32)
                        normed = both[:HEAD] / both[HEAD : HEAD + 1]
                        os[at, h * HEAD : (h + 1) * HEAD] = normed.T.astype(jnp.bfloat16)

        run_copies(
            [
                (os.at[pl.ds(pl.multiple_of((j ^ d) * rows, rows), rows), :], outs[d])
                for d in range(LEVEL)
            ],
            out_sems,
        )

    bf = jnp.bfloat16
    bias, onehot, ranges = tables
    return pl.pallas_call(
        kernel,
        out_shape=[jax.ShapeDtypeStruct((rows, width), bf)] * LEVEL,
        in_specs=[SMEM] + [HBM] * (2 * LEVEL + 6),
        out_specs=[HBM] * LEVEL,
        scratch_shapes=[
            pltpu.VMEM((key_rows, width), bf),
            pltpu.VMEM((key_rows, width), bf),
            pltpu.VMEM((heads, HEAD + 16, key_rows), bf),
            pltpu.VMEM((LEVEL * rows, width), bf),
            pltpu.VMEM((LEVEL * rows, width), bf),
            pltpu.VMEM((key_rows, lanes), bf),
            pltpu.VMEM((LEVEL * rows, lanes), bf),
            pltpu.SemaphoreType.DMA((n_copies,)),
            pltpu.SemaphoreType.DMA((LEVEL,)),
        ],
        cost_estimate=cost(4 * key_rows * width, 8 * LEVEL * rows * 1024 * width),
        name="attention",
    )(ranges, bias, onehot, queries, own, *swapped, *q_swapped, *own_far, *far)


def gather_out(pieces, rows, slab, dtype):
    def kernel(*refs):
        ins, out, sems = refs[:-2], refs[-2], refs[-1]
        j = lax.rem(lax.axis_index("ctx"), LEVEL)
        pairs, offset = [], 0
        for g, heads in enumerate(SPLIT):
            width = heads * HEAD
            for d in range(LEVEL):
                c = pl.multiple_of((j ^ d) * slab + offset, HEAD)
                pairs.append((ins[g * LEVEL + d], out.at[:, pl.ds(c, width)]))
            offset += width
        run_copies(pairs, sems)

    return pl.pallas_call(
        kernel,
        out_shape=jax.ShapeDtypeStruct((rows, LEVEL * slab), dtype),
        in_specs=[HBM] * len(pieces),
        out_specs=VMEM,
        scratch_shapes=[pltpu.SemaphoreType.DMA((len(pieces),))],
        cost_estimate=cost(4 * rows * LEVEL * slab),
        name="gather_out",
    )(*pieces)


def attend(queries, key_states, value_states, stretch_lengths, stretch_mask):
    rows, features = queries.shape
    slab = features // LEVEL
    ahead = (MAXLEN - 2) // rows + 1
    assert LEVEL * rows >= (WIN + 1) * MAXLEN - 1 and ahead < LEVEL
    assert sum(SPLIT) * HEAD == slab
    assert (WIN + 2) * MAXLEN + rows + HEAD <= SIZES[-1] * TILE + 4
    widths = [heads * HEAD for heads in SPLIT]
    offsets = [sum(widths[:g]) for g in range(len(widths))]
    groups = range(len(SPLIT))
    arrays = (key_states, value_states, queries)
    tables = lookup_tables(stretch_lengths, stretch_mask, rows, 2 * LEVEL + ahead)

    def spans(kinds, g):
        return [(i, slab, offsets[g], widths[g]) for i in kinds]

    messages = [spans((0, 1), 0)]
    messages += [spans((0, 1), g) + spans((2,), g - 1) for g in groups[1:]]
    messages += [spans((2,), groups[-1])]
    own_spans = [span for g in groups for span in spans((0, 1), g)]
    jobs = [(d, messages[0]) for d in OTHERS] + [(0, own_spans)]
    *parts, own = pack_columns(arrays, jobs)
    jobs = [(d, message) for message in messages[1:] for d in OTHERS]
    parts += pack_columns(arrays, jobs)
    swapped, far = [], []
    for m in range(len(messages)):
        mine = parts[m * len(OTHERS) : (m + 1) * len(OTHERS)]
        swapped.append([swap(x, d) for x, d in zip(mine, OTHERS)])
    own_far = [swap_levels(own, p) for p in range(2)]
    for g in groups:
        sides = pack_z(own, swapped[g], ahead, 2 * offsets[g], widths[g])
        far.append([swap_levels(x, p) for p, x in enumerate(sides)])
    pieces = []
    for g in groups:
        outs = attention(
            tables, queries, own, swapped[g], swapped[g + 1], own_far, far[g], ahead,
            offsets[g], widths[g], 2 * widths[g + 1] if g < groups[-1] else 0, slab,
        )
        pieces += [outs[0]]
        pieces += [swap(outs[d], d) for d in OTHERS]
    return gather_out(pieces, rows, slab, queries.dtype)


def solution(mesh):
    rows = P(("groups", "ctx"), None)
    in_specs = (rows, rows, rows, P("groups"), P("groups", None))
    return jax.shard_map(attend, mesh=mesh, in_specs=in_specs, out_specs=rows, check_vma=False)
```

```python
import math

import jax
import jax.numpy as jnp
from jax import lax
from jax.experimental import pallas as pl
from jax.experimental.pallas import tpu as pltpu
from jax.sharding import PartitionSpec as P


HEAD = 128
MAXLEN = 512
WIN = 1
LEVEL = 4
SPLIT = (2, 2, 2)
OTHERS = tuple(range(1, LEVEL))
NEG = -1e30
TILE = 256
SIZES = (2, 3, 4, 5, 6, 8)
ANY = pl.BlockSpec(memory_space=pl.ANY)
VMEM = pl.BlockSpec(memory_space=pltpu.VMEM)
SMEM = pl.BlockSpec(memory_space=pltpu.SMEM)


def swap(value, bits):
    return lax.ppermute(value, "ctx", [(i, i ^ bits) for i in range(lax.axis_size("ctx"))])


def swap_levels(value, parity):
    count = lax.axis_size("ctx")
    pairs = {i: i ^ 1 for i in range(count)}
    for low in range(parity * LEVEL, count - LEVEL, 2 * LEVEL):
        for i in range(low, low + LEVEL):
            pairs[i], pairs[i + LEVEL] = i + LEVEL, i
    return lax.ppermute(value, "ctx", sorted(pairs.items()))


def run_copies(pairs, sems):
    copies = [pltpu.make_async_copy(a, b, sems.at[n]) for n, (a, b) in enumerate(pairs)]
    for c in copies:
        c.start()
    for c in copies:
        c.wait()


def cost(nbytes, flops=0):
    return pl.CostEstimate(flops=flops, bytes_accessed=nbytes, transcendentals=0)


def vmem(mebibytes):
    return pltpu.CompilerParams(vmem_limit_bytes=mebibytes << 20)


def pack_columns(arrays, jobs, limit):
    rows = arrays[0].shape[0]
    totals = [sum(span[3] for span in spans) for _, spans in jobs]

    def kernel(*refs):
        ins, outs, sems = refs[: len(arrays)], refs[len(arrays) : -1], refs[-1]
        j = lax.rem(lax.axis_index("ctx"), LEVEL)
        pairs = []
        for out, (d, spans) in zip(outs, jobs):
            to = 0
            for which, unit, offset, width in spans:
                c = pl.multiple_of((j ^ d) * unit + offset, 128)
                pairs.append((ins[which].at[:, pl.ds(c, width)], out.at[:, pl.ds(to, width)]))
                to += width
        run_copies(pairs, sems)

    return pl.pallas_call(
        kernel,
        out_shape=[jax.ShapeDtypeStruct((rows, total), arrays[0].dtype) for total in totals],
        in_specs=[ANY] * len(arrays),
        out_specs=[VMEM] * len(jobs),
        scratch_shapes=[pltpu.SemaphoreType.DMA((sum(len(spans) for _, spans in jobs),))],
        cost_estimate=cost(4 * rows * sum(totals)),
        compiler_params=vmem(limit),
    )(*arrays)


def pack_z(own, swapped, ahead, offset, width):
    rows = own.shape[0]
    n_fwd = LEVEL - 1

    def kernel(o, *rest):
        outs, sems = rest[LEVEL - 1 : -1], rest[-1]
        pieces = [o.at[:, pl.ds(offset, 2 * width)]]
        pieces += [ref.at[:, pl.ds(0, 2 * width)] for ref in rest[: LEVEL - 1]]
        me = lax.axis_index("ctx")
        j = lax.rem(me, LEVEL)
        odd = lax.rem(me // LEVEL, 2)
        for parity in range(2):
            fwd, back = outs[parity], outs[1 - parity]

            @pl.when(odd == parity)
            def _():
                for d in range(1, LEVEL):
                    pltpu.make_async_copy(pieces[d], fwd.at[d - 1], sems.at[d - 1]).start()
                for b in range(ahead):
                    for d in range(LEVEL):
                        @pl.when((j ^ b) == d)
                        def _():
                            pltpu.make_async_copy(
                                pieces[d], back.at[b], sems.at[n_fwd + b]
                            ).start()
        for n in range(n_fwd + ahead):
            pltpu.make_async_copy(pieces[0], outs[0].at[0], sems.at[n]).wait()

    return pl.pallas_call(
        kernel,
        out_shape=[jax.ShapeDtypeStruct((n_fwd, rows, 2 * width), own.dtype)] * 2,
        in_specs=[ANY] * LEVEL,
        out_specs=[VMEM, VMEM],
        scratch_shapes=[pltpu.SemaphoreType.DMA((n_fwd + ahead,))],
        cost_estimate=cost(8 * rows * width * (n_fwd + ahead)),
        compiler_params=vmem(8),
        name="pack_z",
    )(own, *swapped)


def lookup_tables(lengths, mask, rows, key_blocks):
    stretches = lengths.shape[0]
    lanes = -(-stretches // HEAD) * HEAD
    key_rows, query_rows = key_blocks * rows, LEVEL * rows

    def kernel(len_ref, mask_ref, bias, onehot, ranges):
        base = (lax.axis_index("ctx") // LEVEL - 1) * query_rows
        lane = lax.broadcasted_iota(jnp.int32, (1, lanes), 1)
        for b in range(LEVEL):
            ranges[b, 0] = jnp.int32(0)
            ranges[b, 1] = jnp.int32(0)

        def scan(a, carry):
            start, before, own, lo, hi = carry
            length = len_ref[a]
            back = jnp.where(mask_ref[a, jnp.maximum(a - 1, 0)] > 0, before, 0)
            end = start + length
            here = lane == a
            for b in range(LEVEL):
                first = (LEVEL + b) * rows
                ranges[b, 0] = jnp.where(start <= first, start - back, ranges[b, 0])
                ranges[b, 1] = jnp.where(start < first + rows, end, ranges[b, 1])
            return (
                end,
                length,
                jnp.where(here, start, own),
                jnp.where(here, start - back, lo),
                jnp.where(here, end, hi),
            )

        zero = jnp.full((1, lanes), -(1 << 30), jnp.int32)
        _, _, own, lo, hi = lax.fori_loop(
            0, stretches, scan, (-base, jnp.int32(0), zero, zero, zero)
        )
        for b in range(LEVEL):
            start = jnp.maximum(ranges[b, 0], 0) // HEAD * HEAD
            tiles = jnp.int32(SIZES[-1])
            for size in SIZES[-2::-1]:
                tiles = jnp.where(ranges[b, 1] - start <= size * TILE, size, tiles)
            ranges[b, 0] = jnp.minimum(start, key_rows - tiles * TILE)
            ranges[b, 1] = tiles
        low, high = jnp.int32(key_rows), jnp.int32(0)
        for b in range(LEVEL):
            low = jnp.minimum(low, ranges[b, 0])
            high = jnp.maximum(high, ranges[b, 0] + ranges[b, 1] * TILE)
        ranges[LEVEL, 0] = low // rows
        ranges[LEVEL, 1] = (high + rows - 1) // rows

        @pl.loop(0, key_blocks)
        def _(i):
            at = pl.ds(pl.multiple_of(i * rows, rows), rows)
            pos = lax.broadcasted_iota(jnp.int32, (rows, lanes), 0) + i * rows
            inside = (pos >= lo) & (pos < hi)
            bias[at, :] = jnp.where(inside, 0.0, NEG).astype(bias.dtype)

        @pl.loop(0, LEVEL)
        def _(i):
            at = pl.ds(pl.multiple_of(i * rows, rows), rows)
            pos = lax.broadcasted_iota(jnp.int32, (rows, lanes), 0) + (LEVEL + i) * rows
            onehot[at, :] = jnp.where((pos >= own) & (pos < hi), 1.0, 0.0).astype(onehot.dtype)

    bf = jnp.bfloat16
    return pl.pallas_call(
        kernel,
        out_shape=[
            jax.ShapeDtypeStruct((key_rows, lanes), bf),
            jax.ShapeDtypeStruct((query_rows, lanes), bf),
            jax.ShapeDtypeStruct((LEVEL + 1, 2), jnp.int32),
        ],
        in_specs=[SMEM, SMEM],
        out_specs=[VMEM, VMEM, SMEM],
        cost_estimate=cost(2 * (key_rows + query_rows) * lanes),
        compiler_params=vmem(8),
        name="lookup_tables",
    )(lengths, mask)


def attention(
    tables, queries, own, swapped, q_swapped, own_far, far, ahead, offset, width, q_offset, slab
):
    rows = queries.shape[0]
    heads = width // HEAD
    key_blocks = 2 * LEVEL + ahead
    key_rows = key_blocks * rows
    lanes = tables[0].shape[1]
    factor = math.log2(math.e) / math.sqrt(HEAD)
    n_copies = 2 * key_blocks + 2 + LEVEL

    def kernel(ranges, bias_hbm, onehot_hbm, q, *rest):
        level, rest = rest[:LEVEL], rest[LEVEL:]
        asked, rest = rest[: LEVEL - 1], rest[LEVEL - 1 :]
        own_sides, sides, rest = rest[:2], rest[2:4], rest[4:]
        outs, scratch = rest[:LEVEL], rest[LEVEL:]
        ks, vs, vt, qs, os, bias, onehot, sems, out_sems = scratch
        me = lax.axis_index("ctx")
        j = lax.rem(me, LEVEL)
        odd = lax.rem(me // LEVEL, 2)

        def kv(src, block, off=0):
            at = pl.ds(pl.multiple_of(block * rows, rows), rows)
            value = pltpu.make_async_copy(
                src.at[:, pl.ds(off + width, width)], vs.at[at, :], sems.at[block]
            )
            key = pltpu.make_async_copy(
                src.at[:, pl.ds(off, width)], ks.at[at, :], sems.at[key_blocks + block]
            )
            return [value, key]

        def level_copies():
            copies = []
            for d in range(LEVEL):
                copies += kv(level[d], LEVEL + (j ^ d), 2 * offset if d == 0 else 0)
            return copies

        rest_pairs = [(bias_hbm, bias), (onehot_hbm, onehot)]
        for d in range(LEVEL):
            at = pl.ds(pl.multiple_of((j ^ d) * rows, rows), rows)
            if d == 0:
                c = pl.multiple_of(j * slab + offset, HEAD)
                rest_pairs.append((q.at[:, pl.ds(c, width)], qs.at[at, :]))
            else:
                rest_pairs.append((asked[d - 1].at[:, pl.ds(q_offset, width)], qs.at[at, :]))

        def side_copies(parity):
            behind, front = 1 - parity, parity
            out = kv(own_sides[behind], j, 2 * offset)
            for d in range(1, LEVEL):
                out += kv(sides[behind].at[d - 1], j ^ d)
            for b in range(ahead):
                out += kv(sides[front].at[b], 2 * LEVEL + b)
            return out

        near = level_copies()
        rest = [
            pltpu.make_async_copy(a, b, sems.at[2 * key_blocks + n])
            for n, (a, b) in enumerate(rest_pairs)
        ]
        for part in range(2):
            for c in near[part::2]:
                c.start()
            for parity in range(2):
                @pl.when(odd == parity)
                def _():
                    for c in side_copies(parity)[part::2]:
                        c.start()
        for c in rest:
            c.start()
        for h in range(heads):
            vt[h, HEAD:, :] = jnp.ones_like(vt[h, HEAD:, :])

        @pl.loop(0, key_blocks)
        def _(i):
            at = pl.ds(pl.multiple_of(i * rows, rows), rows)
            pltpu.make_async_copy(ks.at[at, :], vs.at[at, :], sems.at[i]).wait()

            @pl.when((i >= ranges[LEVEL, 0]) & (i < ranges[LEVEL, 1]))
            def _():
                for h in range(heads):
                    vt[h, :HEAD, at] = vs[at, h * HEAD : (h + 1) * HEAD].T

        @pl.loop(0, key_blocks)
        def _(i):
            at = pl.ds(pl.multiple_of(i * rows, rows), rows)
            pltpu.make_async_copy(vs.at[at, :], ks.at[at, :], sems.at[key_blocks + i]).wait()

        for c in rest:
            c.wait()

        @pl.loop(0, LEVEL)
        def _(b):
            at = pl.ds(pl.multiple_of(b * rows, rows), rows)
            start = pl.multiple_of(ranges[b, 0], HEAD)
            for size in SIZES:
                @pl.when(ranges[b, 1] == size)
                def _():
                    k_at = pl.ds(start, size * TILE)
                    scores = [
                        lax.dot_general(
                            jnp.concatenate(
                                [ks[k_at, h * HEAD : (h + 1) * HEAD], bias[k_at, :]], axis=1
                            ),
                            jnp.concatenate(
                                [qs[at, h * HEAD : (h + 1) * HEAD], onehot[at, :]], axis=1
                            ),
                            (((1,), (1,)), ((), ())),
                            preferred_element_type=jnp.float32,
                        )
                        for h in range(heads)
                    ]
                    for h, s in enumerate(scores):
                        top = jnp.max(s, axis=0, keepdims=True)
                        p = jnp.exp2((s - top) * factor).astype(jnp.bfloat16)
                        both = jnp.dot(vt[h, :, k_at], p, preferred_element_type=jnp.float32)
                        normed = both[:HEAD] / both[HEAD : HEAD + 1]
                        os[at, h * HEAD : (h + 1) * HEAD] = normed.T.astype(jnp.bfloat16)

        run_copies(
            [
                (os.at[pl.ds(pl.multiple_of((j ^ d) * rows, rows), rows), :], outs[d])
                for d in range(LEVEL)
            ],
            out_sems,
        )

    bf = jnp.bfloat16
    bias, onehot, ranges = tables
    return pl.pallas_call(
        kernel,
        out_shape=[jax.ShapeDtypeStruct((rows, width), bf)] * LEVEL,
        in_specs=[SMEM] + [ANY] * (2 * LEVEL + 6),
        out_specs=[ANY] * LEVEL,
        scratch_shapes=[
            pltpu.VMEM((key_rows, width), bf),
            pltpu.VMEM((key_rows, width), bf),
            pltpu.VMEM((heads, HEAD + 16, key_rows), bf),
            pltpu.VMEM((LEVEL * rows, width), bf),
            pltpu.VMEM((LEVEL * rows, width), bf),
            pltpu.VMEM((key_rows, lanes), bf),
            pltpu.VMEM((LEVEL * rows, lanes), bf),
            pltpu.SemaphoreType.DMA((n_copies,)),
            pltpu.SemaphoreType.DMA((LEVEL,)),
        ],
        cost_estimate=cost(4 * key_rows * width, 8 * LEVEL * rows * 1024 * width),
        compiler_params=vmem(24),
        name="attention",
    )(ranges, bias, onehot, queries, own, *swapped, *q_swapped, *own_far, *far)


def gather_out(pieces, rows, slab, dtype):
    def kernel(*refs):
        ins, out, sems = refs[:-2], refs[-2], refs[-1]
        j = lax.rem(lax.axis_index("ctx"), LEVEL)
        pairs, offset = [], 0
        for g, heads in enumerate(SPLIT):
            width = heads * HEAD
            for d in range(LEVEL):
                c = pl.multiple_of((j ^ d) * slab + offset, HEAD)
                pairs.append((ins[g * LEVEL + d], out.at[:, pl.ds(c, width)]))
            offset += width
        run_copies(pairs, sems)

    return pl.pallas_call(
        kernel,
        out_shape=jax.ShapeDtypeStruct((rows, LEVEL * slab), dtype),
        in_specs=[ANY] * len(pieces),
        out_specs=VMEM,
        scratch_shapes=[pltpu.SemaphoreType.DMA((len(pieces),))],
        cost_estimate=cost(4 * rows * LEVEL * slab),
        compiler_params=vmem(8),
        name="gather_out",
    )(*pieces)


def attend(queries, key_states, value_states, stretch_lengths, stretch_mask):
    rows, features = queries.shape
    slab = features // LEVEL
    ahead = (MAXLEN - 2) // rows + 1
    assert LEVEL * rows >= (WIN + 1) * MAXLEN - 1 and ahead < LEVEL
    assert sum(SPLIT) * HEAD == slab
    assert (WIN + 2) * MAXLEN + rows + HEAD <= SIZES[-1] * TILE + 4
    widths = [heads * HEAD for heads in SPLIT]
    offsets = [sum(widths[:g]) for g in range(len(widths))]
    groups = range(len(SPLIT))
    arrays = (key_states, value_states, queries)
    tables = lookup_tables(stretch_lengths, stretch_mask, rows, 2 * LEVEL + ahead)

    def spans(kinds, g):
        return [(i, slab, offsets[g], widths[g]) for i in kinds]

    messages = [spans((0, 1), 0)]
    messages += [spans((0, 1), g) + spans((2,), g - 1) for g in groups[1:]]
    messages += [spans((2,), groups[-1])]
    own_spans = [span for g in groups for span in spans((0, 1), g)]
    (own,) = pack_columns(arrays[:2], [(0, own_spans)], 60)
    jobs = [(d, messages[0]) for d in OTHERS]
    parts = pack_columns(arrays[:2], jobs, 60)
    jobs = [(d, message) for message in messages[1:] for d in OTHERS]
    parts += pack_columns(arrays, jobs, 12)
    swapped, far = [], []
    for m in range(len(messages)):
        mine = parts[m * len(OTHERS) : (m + 1) * len(OTHERS)]
        swapped.append([swap(x, d) for x, d in zip(mine, OTHERS)])
    own_far = [swap_levels(own, p) for p in range(2)]
    for g in groups:
        sides = pack_z(own, swapped[g], ahead, 2 * offsets[g], widths[g])
        far.append([swap_levels(x, p) for p, x in enumerate(sides)])
    pieces = []
    for g in groups:
        outs = attention(
            tables, queries, own, swapped[g], swapped[g + 1], own_far, far[g], ahead,
            offsets[g], widths[g], 2 * widths[g + 1] if g < groups[-1] else 0, slab,
        )
        pieces += [outs[0]]
        pieces += [swap(outs[d], d) for d in OTHERS]
    return gather_out(pieces, rows, slab, queries.dtype)


def solution(mesh):
    rows = P(("groups", "ctx"), None)
    in_specs = (rows, rows, rows, P("groups"), P("groups", None))
    return jax.shard_map(attend, mesh=mesh, in_specs=in_specs, out_specs=rows, check_vma=False)
```

```python
import math

import jax
import jax.numpy as jnp
from jax import lax
from jax.experimental import pallas as pl
from jax.experimental.pallas import tpu as pltpu
from jax.sharding import PartitionSpec as P


HEAD = 128
MAXLEN = 512
WIN = 1
LEVEL = 4
SPLIT = (2, 2, 2)
OTHERS = tuple(range(1, LEVEL))
NEG = -1e30
TILE = 128
SIZES = (4, 5, 6, 7, 8, 10, 12, 16)
ANY = pl.BlockSpec(memory_space=pl.ANY)
VMEM = pl.BlockSpec(memory_space=pltpu.VMEM)
SMEM = pl.BlockSpec(memory_space=pltpu.SMEM)


def swap(value, bits):
    return lax.ppermute(value, "ctx", [(i, i ^ bits) for i in range(lax.axis_size("ctx"))])


def swap_levels(value, parity):
    count = lax.axis_size("ctx")
    pairs = {i: i ^ 1 for i in range(count)}
    for low in range(parity * LEVEL, count - LEVEL, 2 * LEVEL):
        for i in range(low, low + LEVEL):
            pairs[i], pairs[i + LEVEL] = i + LEVEL, i
    return lax.ppermute(value, "ctx", sorted(pairs.items()))


def run_copies(pairs, sems):
    copies = [pltpu.make_async_copy(a, b, sems.at[n]) for n, (a, b) in enumerate(pairs)]
    for c in copies:
        c.start()
    for c in copies:
        c.wait()


def cost(nbytes, flops=0):
    return pl.CostEstimate(flops=flops, bytes_accessed=nbytes, transcendentals=0)


def vmem(mebibytes):
    return pltpu.CompilerParams(vmem_limit_bytes=mebibytes << 20)


def pack_columns(arrays, jobs, limit):
    rows = arrays[0].shape[0]
    totals = [sum(span[3] for span in spans) for _, spans in jobs]

    def kernel(*refs):
        ins, outs, sems = refs[: len(arrays)], refs[len(arrays) : -1], refs[-1]
        j = lax.rem(lax.axis_index("ctx"), LEVEL)
        pairs = []
        for out, (d, spans) in zip(outs, jobs):
            to = 0
            for which, unit, offset, width in spans:
                c = pl.multiple_of((j ^ d) * unit + offset, 128)
                pairs.append((ins[which].at[:, pl.ds(c, width)], out.at[:, pl.ds(to, width)]))
                to += width
        run_copies(pairs, sems)

    return pl.pallas_call(
        kernel,
        out_shape=[jax.ShapeDtypeStruct((rows, total), arrays[0].dtype) for total in totals],
        in_specs=[ANY] * len(arrays),
        out_specs=[VMEM] * len(jobs),
        scratch_shapes=[pltpu.SemaphoreType.DMA((sum(len(spans) for _, spans in jobs),))],
        cost_estimate=cost(4 * rows * sum(totals)),
        compiler_params=vmem(limit),
    )(*arrays)


def pack_z(own, swapped, ahead, offset, width):
    rows = own.shape[0]
    n_fwd = LEVEL - 1

    def kernel(o, *rest):
        outs, sems = rest[LEVEL - 1 : -1], rest[-1]
        pieces = [o.at[:, pl.ds(offset, 2 * width)]]
        pieces += [ref.at[:, pl.ds(0, 2 * width)] for ref in rest[: LEVEL - 1]]
        me = lax.axis_index("ctx")
        j = lax.rem(me, LEVEL)
        odd = lax.rem(me // LEVEL, 2)
        for parity in range(2):
            fwd, back = outs[parity], outs[1 - parity]

            @pl.when(odd == parity)
            def _():
                for d in range(1, LEVEL):
                    pltpu.make_async_copy(pieces[d], fwd.at[d - 1], sems.at[d - 1]).start()
                for b in range(ahead):
                    for d in range(LEVEL):
                        @pl.when((j ^ b) == d)
                        def _():
                            pltpu.make_async_copy(
                                pieces[d], back.at[b], sems.at[n_fwd + b]
                            ).start()
        for n in range(n_fwd + ahead):
            pltpu.make_async_copy(pieces[0], outs[0].at[0], sems.at[n]).wait()

    return pl.pallas_call(
        kernel,
        out_shape=[jax.ShapeDtypeStruct((n_fwd, rows, 2 * width), own.dtype)] * 2,
        in_specs=[ANY] * LEVEL,
        out_specs=[VMEM, VMEM],
        scratch_shapes=[pltpu.SemaphoreType.DMA((n_fwd + ahead,))],
        cost_estimate=cost(8 * rows * width * (n_fwd + ahead)),
        compiler_params=vmem(8),
        name="pack_z",
    )(own, *swapped)


def lookup_tables(lengths, mask, rows, key_blocks):
    stretches = lengths.shape[0]
    lanes = -(-stretches // HEAD) * HEAD
    key_rows, query_rows = key_blocks * rows, LEVEL * rows

    def kernel(len_ref, mask_ref, bias, onehot, ranges):
        base = (lax.axis_index("ctx") // LEVEL - 1) * query_rows
        lane = lax.broadcasted_iota(jnp.int32, (1, lanes), 1)
        for b in range(LEVEL):
            ranges[b, 0] = jnp.int32(0)
            ranges[b, 1] = jnp.int32(0)

        def scan(a, carry):
            start, before, own, lo, hi = carry
            length = len_ref[a]
            back = jnp.where(mask_ref[a, jnp.maximum(a - 1, 0)] > 0, before, 0)
            end = start + length
            here = lane == a
            for b in range(LEVEL):
                first = (LEVEL + b) * rows
                ranges[b, 0] = jnp.where(start <= first, start - back, ranges[b, 0])
                ranges[b, 1] = jnp.where(start < first + rows, end, ranges[b, 1])
            return (
                end,
                length,
                jnp.where(here, start, own),
                jnp.where(here, start - back, lo),
                jnp.where(here, end, hi),
            )

        zero = jnp.full((1, lanes), -(1 << 30), jnp.int32)
        _, _, own, lo, hi = lax.fori_loop(
            0, stretches, scan, (-base, jnp.int32(0), zero, zero, zero)
        )
        for b in range(LEVEL):
            start = jnp.maximum(ranges[b, 0], 0) // HEAD * HEAD
            tiles = jnp.int32(SIZES[-1])
            for size in SIZES[-2::-1]:
                tiles = jnp.where(ranges[b, 1] - start <= size * TILE, size, tiles)
            ranges[b, 0] = jnp.minimum(start, key_rows - tiles * TILE)
            ranges[b, 1] = tiles
        low, high = jnp.int32(key_rows), jnp.int32(0)
        for b in range(LEVEL):
            low = jnp.minimum(low, ranges[b, 0])
            high = jnp.maximum(high, ranges[b, 0] + ranges[b, 1] * TILE)
        ranges[LEVEL, 0] = low // rows
        ranges[LEVEL, 1] = (high + rows - 1) // rows

        @pl.loop(0, key_blocks)
        def _(i):
            at = pl.ds(pl.multiple_of(i * rows, rows), rows)
            pos = lax.broadcasted_iota(jnp.int32, (rows, lanes), 0) + i * rows
            inside = (pos >= lo) & (pos < hi)
            bias[at, :] = jnp.where(inside, 0.0, NEG).astype(bias.dtype)

        @pl.loop(0, LEVEL)
        def _(i):
            at = pl.ds(pl.multiple_of(i * rows, rows), rows)
            pos = lax.broadcasted_iota(jnp.int32, (rows, lanes), 0) + (LEVEL + i) * rows
            onehot[at, :] = jnp.where((pos >= own) & (pos < hi), 1.0, 0.0).astype(onehot.dtype)

    bf = jnp.bfloat16
    return pl.pallas_call(
        kernel,
        out_shape=[
            jax.ShapeDtypeStruct((key_rows, lanes), bf),
            jax.ShapeDtypeStruct((query_rows, lanes), bf),
            jax.ShapeDtypeStruct((LEVEL + 1, 2), jnp.int32),
        ],
        in_specs=[SMEM, SMEM],
        out_specs=[VMEM, VMEM, SMEM],
        cost_estimate=cost(2 * (key_rows + query_rows) * lanes),
        compiler_params=vmem(8),
        name="lookup_tables",
    )(lengths, mask)


def attention(
    tables, queries, own, swapped, q_swapped, own_far, far, ahead, offset, width, q_offset, slab
):
    rows = queries.shape[0]
    heads = width // HEAD
    key_blocks = 2 * LEVEL + ahead
    key_rows = key_blocks * rows
    factor = math.log2(math.e) / math.sqrt(HEAD)
    n_copies = 2 * key_blocks + LEVEL

    def kernel(ranges, bias, onehot, q, *rest):
        level, rest = rest[:LEVEL], rest[LEVEL:]
        asked, rest = rest[: LEVEL - 1], rest[LEVEL - 1 :]
        own_sides, sides, rest = rest[:2], rest[2:4], rest[4:]
        outs, scratch = rest[:LEVEL], rest[LEVEL:]
        ks, vs, vt, qs, os, sems, out_sems = scratch
        me = lax.axis_index("ctx")
        j = lax.rem(me, LEVEL)
        odd = lax.rem(me // LEVEL, 2)

        def needed(block):
            return (block >= ranges[LEVEL, 0]) & (block < ranges[LEVEL, 1])

        def fetch(src, block, off=0):
            at = pl.ds(pl.multiple_of(block * rows, rows), rows)

            @pl.when(needed(block))
            def _():
                pltpu.make_async_copy(
                    src.at[:, pl.ds(off + width, width)], vs.at[at, :], sems.at[block]
                ).start()
                pltpu.make_async_copy(
                    src.at[:, pl.ds(off, width)], ks.at[at, :], sems.at[key_blocks + block]
                ).start()

        rest_pairs = []
        for d in range(LEVEL):
            at = pl.ds(pl.multiple_of((j ^ d) * rows, rows), rows)
            if d == 0:
                c = pl.multiple_of(j * slab + offset, HEAD)
                rest_pairs.append((q.at[:, pl.ds(c, width)], qs.at[at, :]))
            else:
                rest_pairs.append((asked[d - 1].at[:, pl.ds(q_offset, width)], qs.at[at, :]))

        rest = [
            pltpu.make_async_copy(a, b, sems.at[2 * key_blocks + n])
            for n, (a, b) in enumerate(rest_pairs)
        ]
        for d in range(LEVEL):
            fetch(level[d], LEVEL + (j ^ d), 2 * offset if d == 0 else 0)
        for parity in range(2):
            @pl.when(odd == parity)
            def _():
                behind, front = 1 - parity, parity
                fetch(own_sides[behind], j, 2 * offset)
                for d in range(1, LEVEL):
                    fetch(sides[behind].at[d - 1], j ^ d)
                for b in range(ahead):
                    fetch(sides[front].at[b], 2 * LEVEL + b)
        for c in rest:
            c.start()
        for h in range(heads):
            vt[h, HEAD:, :] = jnp.ones_like(vt[h, HEAD:, :])

        @pl.loop(0, key_blocks)
        def _(i):
            at = pl.ds(pl.multiple_of(i * rows, rows), rows)

            @pl.when(needed(i))
            def _():
                pltpu.make_async_copy(ks.at[at, :], vs.at[at, :], sems.at[i]).wait()
                for h in range(heads):
                    vt[h, :HEAD, at] = vs[at, h * HEAD : (h + 1) * HEAD].T

        @pl.loop(0, key_blocks)
        def _(i):
            at = pl.ds(pl.multiple_of(i * rows, rows), rows)

            @pl.when(needed(i))
            def _():
                pltpu.make_async_copy(vs.at[at, :], ks.at[at, :], sems.at[key_blocks + i]).wait()

        for c in rest:
            c.wait()

        @pl.loop(0, LEVEL)
        def _(b):
            at = pl.ds(pl.multiple_of(b * rows, rows), rows)
            start = pl.multiple_of(ranges[b, 0], HEAD)
            for size in SIZES:
                @pl.when(ranges[b, 1] == size)
                def _():
                    k_at = pl.ds(start, size * TILE)
                    scores = [
                        lax.dot_general(
                            jnp.concatenate(
                                [ks[k_at, h * HEAD : (h + 1) * HEAD], bias[k_at, :]], axis=1
                            ),
                            jnp.concatenate(
                                [qs[at, h * HEAD : (h + 1) * HEAD], onehot[at, :]], axis=1
                            ),
                            (((1,), (1,)), ((), ())),
                            preferred_element_type=jnp.float32,
                        )
                        for h in range(heads)
                    ]
                    for h, s in enumerate(scores):
                        top = jnp.max(s, axis=0, keepdims=True)
                        p = jnp.exp2((s - top) * factor).astype(jnp.bfloat16)
                        both = jnp.dot(vt[h, :, k_at], p, preferred_element_type=jnp.float32)
                        normed = both[:HEAD] / both[HEAD : HEAD + 1]
                        os[at, h * HEAD : (h + 1) * HEAD] = normed.T.astype(jnp.bfloat16)

        run_copies(
            [
                (os.at[pl.ds(pl.multiple_of((j ^ d) * rows, rows), rows), :], outs[d])
                for d in range(LEVEL)
            ],
            out_sems,
        )

    bf = jnp.bfloat16
    bias, onehot, ranges = tables
    return pl.pallas_call(
        kernel,
        out_shape=[jax.ShapeDtypeStruct((rows, width), bf)] * LEVEL,
        in_specs=[SMEM, VMEM, VMEM] + [ANY] * (2 * LEVEL + 4),
        out_specs=[ANY] * LEVEL,
        scratch_shapes=[
            pltpu.VMEM((key_rows, width), bf),
            pltpu.VMEM((key_rows, width), bf),
            pltpu.VMEM((heads, HEAD + 16, key_rows), bf),
            pltpu.VMEM((LEVEL * rows, width), bf),
            pltpu.VMEM((LEVEL * rows, width), bf),
            pltpu.SemaphoreType.DMA((n_copies,)),
            pltpu.SemaphoreType.DMA((LEVEL,)),
        ],
        cost_estimate=cost(4 * key_rows * width, 8 * LEVEL * rows * 1024 * width),
        compiler_params=vmem(24),
        name="attention",
    )(ranges, bias, onehot, queries, own, *swapped, *q_swapped, *own_far, *far)


def gather_out(pieces, first, rows, slab, dtype, into=None):
    held = () if into is None else (into,)

    def kernel(*refs):
        ins, out, sems = refs[len(held) : -2], refs[-2], refs[-1]
        j = lax.rem(lax.axis_index("ctx"), LEVEL)
        pairs, offset = [], sum(SPLIT[:first]) * HEAD
        for g in range(len(ins) // LEVEL):
            width = SPLIT[first + g] * HEAD
            for d in range(LEVEL):
                c = pl.multiple_of((j ^ d) * slab + offset, HEAD)
                pairs.append((ins[g * LEVEL + d], out.at[:, pl.ds(c, width)]))
            offset += width
        run_copies(pairs, sems)

    return pl.pallas_call(
        kernel,
        out_shape=jax.ShapeDtypeStruct((rows, LEVEL * slab), dtype),
        in_specs=[ANY] * (len(held) + len(pieces)),
        out_specs=ANY,
        input_output_aliases={0: 0} if held else {},
        scratch_shapes=[pltpu.SemaphoreType.DMA((len(pieces),))],
        cost_estimate=cost(4 * rows * LEVEL * slab),
        compiler_params=vmem(8),
        name="gather_out",
    )(*held, *pieces)


def attend(queries, key_states, value_states, stretch_lengths, stretch_mask):
    rows, features = queries.shape
    slab = features // LEVEL
    ahead = (MAXLEN - 2) // rows + 1
    assert LEVEL * rows >= (WIN + 1) * MAXLEN - 1 and ahead < LEVEL
    assert sum(SPLIT) * HEAD == slab
    assert (WIN + 2) * MAXLEN + rows + HEAD <= SIZES[-1] * TILE + 4
    widths = [heads * HEAD for heads in SPLIT]
    offsets = [sum(widths[:g]) for g in range(len(widths))]
    groups = range(len(SPLIT))
    arrays = (key_states, value_states, queries)
    tables = lookup_tables(stretch_lengths, stretch_mask, rows, 2 * LEVEL + ahead)

    def spans(kinds, g):
        return [(i, slab, offsets[g], widths[g]) for i in kinds]

    messages = [spans((0, 1), 0)]
    messages += [spans((0, 1), g) + spans((2,), g - 1) for g in groups[1:]]
    messages += [spans((2,), groups[-1])]
    own_spans = [span for g in groups for span in spans((0, 1), g)]
    (own,) = pack_columns(arrays[:2], [(0, own_spans)], 60)
    jobs = [(d, messages[0]) for d in OTHERS]
    parts = pack_columns(arrays[:2], jobs, 60)
    jobs = [(d, message) for message in messages[1:] for d in OTHERS]
    parts += pack_columns(arrays, jobs, 12)
    swapped, far = [], []
    for m in range(len(messages)):
        mine = parts[m * len(OTHERS) : (m + 1) * len(OTHERS)]
        swapped.append([swap(x, d) for x, d in zip(mine, OTHERS)])
    own_far = [swap_levels(own, p) for p in range(2)]
    for g in groups:
        sides = pack_z(own, swapped[g], ahead, 2 * offsets[g], widths[g])
        far.append([swap_levels(x, p) for p, x in enumerate(sides)])
    pieces = []
    for g in groups:
        outs = attention(
            tables, queries, own, swapped[g], swapped[g + 1], own_far, far[g], ahead,
            offsets[g], widths[g], 2 * widths[g + 1] if g < groups[-1] else 0, slab,
        )
        pieces += [outs[0]]
        pieces += [swap(outs[d], d) for d in OTHERS]
    early = len(pieces) - LEVEL
    out = gather_out(pieces[:early], 0, rows, slab, queries.dtype)
    return gather_out(pieces[early:], len(SPLIT) - 1, rows, slab, queries.dtype, out)


def solution(mesh):
    rows = P(("groups", "ctx"), None)
    in_specs = (rows, rows, rows, P("groups"), P("groups", None))
    return jax.shard_map(attend, mesh=mesh, in_specs=in_specs, out_specs=rows, check_vma=False)
```
